32 devices in a mesh: row: 8 (over y, x, core), col: 4 (over z).
Axes of the slice: x: 2, y: 2, z: 4, core: 2. Of those that a mesh axis runs over, the one named last changes fastest.
Arguments:
- coeffs: bfloat16 [16384, 2048], P('row', 'col'), may hold values from -0.8984375 to 0.8984375
- occupations: float32 [2048], replicated, may hold values from 0.05 to 2
- block_order: int32 [32], replicated, may hold values from 0 to 31, as said below
- neighbours: int32 [32, 15], P(('row', 'col')), may hold values from 0 to 31, as said below
- counts: int32 [32], P(('row', 'col')), may hold values from 4 to 15, as said below
Outputs:
- density: bfloat16 [32, 15, 512, 512], P(('row', 'col'))
The draws below stay inside these ranges and needn't reach their ends.
Inputs may be any that keep to these rules, and one draw needn't show every extreme that they name: Within each aligned group of 4 entries, block_order is a permutation of that group's own indices. For atom row block a, the first counts[a] entries of neighbours[a] are distinct blocks b with |b - a| < 8; the remaining entries equal a. `counts`: some block has 15 live slots in every draw.
All inputs are finite; a program needn't handle non-finite values.
Results may differ from the reference program's by a relative error of at most 0.0044.
Values may be sent and summed in bfloat16 or wider, within the bound.
A program may use at most 128 MiB of HBM per device.

```python
import jax
import jax.numpy as jnp
from jax import lax

BS = 512
STATES = 2048
W = 8
NNB = 15
NBLK = 32
NB = 16384
N_COL = 4


def pattern_draw(key):
    base = jax.random.fold_in(key, 71)
    offsets = jnp.arange(NNB, dtype=jnp.int32) - (W - 1)
    row_keys = jax.random.split(jax.random.fold_in(base, 1), NBLK)
    shuffled = jax.vmap(lambda k: jax.random.permutation(k, offsets))(row_keys)
    blocks = jnp.arange(NBLK, dtype=jnp.int32)
    targets = blocks[:, None] + shuffled
    valid = (targets >= 0) & (targets < NBLK) & (shuffled != 0)
    ranks = jnp.argsort(jnp.where(valid, 0, 1).astype(jnp.int32), axis=1, stable=True)
    targets = jnp.take_along_axis(targets, ranks, axis=1)
    available = jnp.sum(valid.astype(jnp.int32), axis=1) + 1
    wanted = jax.random.randint(jax.random.fold_in(base, 2), (NBLK,), 4, NNB + 1).astype(jnp.int32)
    heavy = jax.random.randint(jax.random.fold_in(base, 3), (), W, NBLK - W + 1).astype(jnp.int32)
    wanted = jnp.where(blocks == heavy, NNB, wanted)
    live = jnp.minimum(wanted, available)
    own_first = jnp.concatenate([blocks[:, None], targets[:, :NNB - 1]], axis=1)
    slots = jnp.arange(NNB, dtype=jnp.int32)[None, :]
    lists = jnp.where(slots < live[:, None], own_first, blocks[:, None])
    return (lists.astype(jnp.int32), live.astype(jnp.int32))


def draw_neighbours(key, part):
    return pattern_draw(key)[0]


def draw_counts(key, part):
    return pattern_draw(key)[1]


def draw_block_order(key, part):
    group_keys = jax.random.split(jax.random.fold_in(key, 5), NBLK // N_COL)
    perms = jax.vmap(lambda k: jax.random.permutation(k, N_COL))(group_keys).astype(jnp.int32)
    bases = (jnp.arange(NBLK // N_COL, dtype=jnp.int32) * N_COL)[:, None]
    return (perms + bases).reshape(NBLK).astype(jnp.int32)


def level_of(key, shape, shards, smallest, high):
    def one(position, shards_of):
        heights = jax.random.uniform(jax.random.fold_in(jax.random.fold_in(key, 6), position), (shards_of,), jnp.float32, smallest / len(shards), high / len(shards))
        return jnp.repeat(jnp.exp(heights), shape[position] // shards_of).reshape((-1,) + (1,) * (len(shape) - position - 1))

    factor_of = one(*shards[0])
    for cut in shards[1:]:
        factor_of = factor_of * one(*cut)
    return factor_of


def noise(key, extent, scale, bound, cuts=(), kind=jnp.bfloat16):
    values = scale * jax.random.normal(key, extent, jnp.float32)
    if cuts:
        values = values * level_of(key, extent, cuts, -0.22, 0.18)
    return jnp.clip(values, -bound, bound).astype(kind)


def setup_inputs(seed: int = 0) -> dict:
    keys = jax.random.split(jax.random.key(seed), 6)
    coeffs = noise(keys[0], (NB, STATES), 0.15, 0.8984375, ((0, 8), (1, 4)))
    occupations = jnp.clip(jax.random.uniform(keys[1], (STATES,), jnp.float32, 0.05, 2.0), 0.05, 2.0)
    block_order = draw_block_order(jax.random.fold_in(keys[5], 71), 0)
    neighbours = draw_neighbours(jax.random.fold_in(keys[5], 71), 0)
    counts = draw_counts(jax.random.fold_in(keys[5], 71), 0)
    return dict(coeffs=coeffs, occupations=occupations, block_order=block_order, neighbours=neighbours, counts=counts)


def reference(coeffs, occupations, block_order, neighbours, counts):
    atoms = coeffs.reshape(NBLK, BS, STATES)[block_order.astype(jnp.int32)]
    weighted = (atoms.astype(jnp.float32) * occupations[None, None, :]).astype(jnp.bfloat16)
    slots = jnp.arange(NNB, dtype=jnp.int32)

    def one_block(items):
        weight_rows, partner, live_count = items
        chosen = atoms[partner.astype(jnp.int32)].astype(jnp.float32)
        products = jnp.einsum("ik,jnk->jin", weight_rows.astype(jnp.float32), chosen)
        live = (slots < live_count)[:, None, None]
        return jnp.where(live, products, jnp.zeros_like(products)).astype(jnp.bfloat16)

    return lax.map(one_block, (weighted, neighbours, counts))
```

```python
import functools

import jax
import jax.numpy as jnp
from jax import lax
from jax.experimental import pallas as pl
from jax.experimental.pallas import tpu as pltpu
from jax.sharding import PartitionSpec as P

W = 8
HALVES = 2
MESH = pl.DeviceIdType.MESH


def kernel(rows, cols, per, own_ref, order_ref, occ_ref, out_ref, stage, gat, raw, wgt, res, in_sem, fsem, psem, rsem, xsem, ysem, usem, osem, qsem):
    row, z = lax.axis_index("row"), lax.axis_index("col")
    k = lax.rem(row, per)
    base = row - k
    place = k * cols + z
    size = per * cols
    halves = raw.shape[1]
    units = cols * halves
    mid = cols // 2
    has_up, has_down = row + per < rows, row >= per
    has_up2, has_down2 = row + 2 * per < rows, row >= 2 * per
    odd = lax.rem(row // per, 2) == 1
    ships_up = has_up & jnp.logical_not(odd) & ((place > 0) | has_down)
    ships_down = has_down & jnp.where(odd, (place < size - 1) | has_up, (place < size - 1) & jnp.logical_not(has_up))
    relays_up = has_up2 & (place > 0) & jnp.logical_not(odd)
    relays_down = has_down2 & (place < size - 1) & odd
    lower, upper = has_down & (place > 0), has_up & (place < size - 1)
    edge = (z == 0) | (z == cols - 1)
    own_done = (jnp.minimum(z, cols - 1 - z) + 1) * halves - 1
    relay_step = jnp.minimum(jnp.where(edge, own_done, own_done + 1), units - 2)
    away_step = relay_step + 1

    def remote(src, dst, send, recv, device):
        return pltpu.make_async_remote_copy(
            src_ref=src, dst_ref=dst, send_sem=send, recv_sem=recv, device_id=device, device_id_type=MESH
        )

    def onward(way, v, c):
        there = lax.rem(z + 1 - 2 * way + cols, cols)
        return remote(gat.at[k, v, c], gat.at[k, v, c], fsem.at[way, v, c], rsem.at[k, v, c], (row, there))

    def partner(d, v, c):
        there = base + lax.rem(k + d, per)
        return remote(gat.at[k, v, c], gat.at[k, v, c], psem.at[d - 1, v, c], rsem.at[k, v, c], (there, z))

    def ship(way, h, c):
        there = lax.rem(row + (1 - 2 * way) * per + rows, rows)
        return remote(gat.at[k, z * halves + h, c], raw.at[way, h, c], xsem.at[way, h, c], usem.at[way, h, c], (there, z))

    def relay(way, h, c):
        there = lax.rem(row + (2 - 4 * way) * per + 2 * rows, rows)
        return remote(raw.at[1 - way, h, c], raw.at[way, h, c], ysem.at[h, c], usem.at[way, h, c], (there, z))

    def taken(way, h, c):
        remote(raw.at[way, h, c], raw.at[way, h, c], xsem.at[0, 0, 0], usem.at[way, h, c], (row, z)).wait_recv()

    def arrive(kk, v, c):
        remote(gat.at[kk, v, c], gat.at[kk, v, c], fsem.at[0, 0, 0], rsem.at[kk, v, c], (row, z)).wait_recv()

    def ship_on(h, c, act):
        @pl.when(ships_up)
        def _():
            act(ship(0, h, c))

        @pl.when(ships_down)
        def _():
            act(ship(1, h, c))

    def start(copy):
        copy.start()

    def sent(copy):
        copy.wait_send()

    fill = pltpu.make_async_copy(own_ref, stage, in_sem)
    fill.start()
    barrier = pltpu.get_barrier_semaphore()
    for d in range(1, per):
        pl.semaphore_signal(barrier, inc=1, device_id=(base + lax.rem(k + d, per), z), device_id_type=MESH)

    greeted = per - 1
    for present, step in ((z < cols - 1, 1), (z > 0, -1)):
        greeted = greeted + present.astype(jnp.int32)

        @pl.when(present)
        def _():
            pl.semaphore_signal(barrier, inc=1, device_id=(row, lax.rem(z + step + cols, cols)), device_id_type=MESH)

    for present, step in ((has_up, per), (has_down, -per), (has_up2, 2 * per), (has_down2, -2 * per)):
        greeted = greeted + present.astype(jnp.int32)

        @pl.when(present)
        def _():
            there = lax.rem(row + step + 2 * rows, rows)
            pl.semaphore_signal(barrier, inc=1, device_id=(there, z), device_id_type=MESH)

    fill.wait()

    first = row * cols

    @pl.loop(0, cols)
    def _(i):
        pick = jnp.clip(order_ref[first + i] - first, 0, cols - 1)

        @pl.loop(0, halves)
        def _(h):
            rows_of = stage.shape[1] // halves
            gat[k, i * halves + h, z] = stage[pick, pl.ds(pl.multiple_of(h * rows_of, rows_of), rows_of)]

    pl.semaphore_wait(barrier, greeted)

    def early(n):
        return 2 * n < units - 1

    def due(way, v, n):
        if way == 0:
            return (z < cols - 1) & jnp.where(z + 1 >= mid, v == units - 1 - n, early(n))
        return (z > 0) & jnp.where(z - 1 < mid, v == n, early(n))

    def awaited(way, v, n):
        if way == 0:
            return jnp.where(z >= mid, v == units - 1 - n, early(n))
        return jnp.where(z < mid, v == n, early(n))

    def own_sends(way, m):
        for v in (units - 1 - m, m) if way == 0 else (m, units - 1 - m):

            @pl.when(due(way, v, m))
            def _():
                onward(way, v, z).start()

    ahead = (jnp.where(z == 0, units, z), jnp.where(z == cols - 1, units, cols - 1 - z))
    for way in (0, 1):

        @pl.loop(0, jnp.minimum(ahead[way], units))
        def _(m):
            own_sends(way, m)

    @pl.loop(0, halves)
    def _(h):
        ship_on(h, z, start)

    @pl.loop(0, units)
    def _(v):
        for d in range(1, per):
            partner(d, v, z).start()

    def got(v, c):
        arrive(k, v, c)
        for d in range(1, per):
            partner(d, v, c).start()

        @pl.when(v // halves == z)
        def _():
            ship_on(lax.rem(v, halves), c, start)

    def gather(n):
        for way in (0, 1):

            @pl.when(n + ahead[way] < units)
            def _():
                own_sends(way, n + ahead[way])

        @pl.loop(1, cols)
        def _(s):
            for way, v in ((0, units - 1 - n), (1, n), (0, n), (1, units - 1 - n)):
                c = z - s if way == 0 else z + s
                there = c >= 0 if way == 0 else c < cols

                @pl.when(there & awaited(way, v, n))
                def _():
                    got(v, c)

                @pl.when(there & due(way, v, n))
                def _():
                    onward(way, v, c).start()

    def relay_on(h, c, act):
        @pl.when(relays_up)
        def _():
            act(relay(0, h, c), 1)

        @pl.when(relays_down)
        def _():
            act(relay(1, h, c), 0)

    def receive_and_relay(h, c):
        def act(copy, way):
            taken(way, h, c)
            copy.start()

        relay_on(h, c, act)

    def relay_all():
        @pl.loop(0, halves)
        def _(h):
            receive_and_relay(h, z)

            @pl.loop(1, cols)
            def _(s):
                @pl.when(z - s >= 0)
                def _():
                    receive_and_relay(h, z - s)

                @pl.when(z + s < cols)
                def _():
                    receive_and_relay(h, z + s)

    def scale(way, source):
        rows_of = wgt.shape[2] // halves
        for h in range(halves):

            @pl.loop(0, cols)
            def _(c):
                wgt[way, c, h * rows_of : (h + 1) * rows_of] = (source(h, c).astype(jnp.float32) * occ_ref[c]).astype(jnp.bfloat16)

    def prepare_away():
        for way, present, waited in ((0, lower, relays_down), (1, upper, relays_up)):

            @pl.when(present)
            def _():
                @pl.when(jnp.logical_not(waited))
                def _():
                    @pl.loop(0, halves)
                    def _(h):
                        @pl.loop(0, cols)
                        def _(c):
                            taken(way, h, c)

                scale(way, lambda h, c: raw[way, h, c])

    def prepare_home():
        scale(2, lambda h, c: gat[k, z * halves + h, c])

    def answer(t):
        low = t < place
        other = jnp.where(low, t, t + 1)
        slot = jnp.where(low, size + other - place, other - place - size) + W - 1
        near = (slot >= 0) & (slot < 2 * W - 1)
        return low, other, slot, near

    def reply(t, h):
        low, other, slot, near = answer(t)
        there = lax.rem(jnp.where(low, row - per, row + per) + rows, rows)
        go = near & jnp.where(low, row - per >= 0, row + per < rows)
        slot = jnp.clip(slot, 0, 2 * W - 2)
        return go, remote(res.at[t, h], out_ref.at[slot, h], osem.at[t, h], qsem.at[slot, h], (there, z))

    def local(t, h):
        other = t - (size - 1)
        slot = other - place + W - 1
        near = (slot >= 0) & (slot < 2 * W - 1)
        slot = jnp.clip(slot, 0, 2 * W - 2)
        return near, pltpu.make_async_copy(res.at[t, h], out_ref.at[slot, h], osem.at[t, h])

    def product(t, way, kk, v):
        total = jnp.zeros(res.shape[2:], jnp.float32)
        for c in range(cols):
            total = total + lax.dot_general(
                wgt[way, c], gat[kk, v, c], (((1,), (1,)), ((), ())), preferred_element_type=jnp.float32
            )
        res[t, lax.rem(v, halves)] = total.astype(jnp.bfloat16)

    def home(kk, v):
        t = kk * cols + v // halves + size - 1
        near, copy = local(t, lax.rem(v, halves))

        @pl.when(near)
        def _():
            product(t, 2, kk, v)
            copy.start()

    def away(kk, v):
        other = kk * cols + v // halves
        low = other < place
        t = jnp.clip(jnp.where(low, other, other - 1), 0, size - 2)
        go, copy = reply(t, lax.rem(v, halves))

        @pl.when(go & (other != place))
        def _():
            product(t, jnp.where(low, 0, 1), kk, v)
            copy.start()

    def unit(n):
        return jnp.where(z < mid, n, units - 1 - n)

    def work(n, since, prepare, each):
        @pl.when(n == since)
        def _():
            prepare()

        @pl.when(n >= since)
        def _():
            @pl.loop(jnp.where(n == since, 0, n), n + 1)
            def _(m):
                @pl.loop(0, per)
                def _(kk):
                    each(kk, unit(m))

    @pl.loop(0, units)
    def _(n):
        gather(n)
        for d in range(1, per):
            kk = lax.rem(k + d, per)

            @pl.loop(0, cols)
            def _(c):
                arrive(kk, unit(n), c)

        work(n, away_step, prepare_away, away)
        work(n, own_done, prepare_home, home)

        @pl.when(n == relay_step)
        def _():
            relay_all()

    @pl.loop(0, units)
    def _(v):
        @pl.loop(0, cols)
        def _(c):
            @pl.when((z < cols - 1) & (c <= z))
            def _():
                onward(0, v, c).wait_send()

            @pl.when((z > 0) & (c >= z))
            def _():
                onward(1, v, c).wait_send()

            for d in range(1, per):
                partner(d, v, c).wait_send()

    @pl.loop(0, halves)
    def _(h):
        @pl.loop(0, cols)
        def _(c):
            ship_on(h, c, sent)
            relay_on(h, c, lambda copy, way: sent(copy))

        @pl.loop(0, size - 1)
        def _(t):
            go, copy = reply(t, h)

            @pl.when(go)
            def _():
                copy.wait_send()

            low, other, slot, near = answer(t)
            arrives = near & jnp.where(low, row + per < rows, row - per >= 0)
            slot = jnp.clip(slot, 0, 2 * W - 2)

            @pl.when(arrives)
            def _():
                remote(res.at[t, h], out_ref.at[slot, h], osem.at[t, h], qsem.at[slot, h], (row, z)).wait_recv()

        @pl.loop(size - 1, 2 * size - 1)
        def _(t):
            near, copy = local(t, h)

            @pl.when(near)
            def _():
                copy.wait()


def place_blocks(neighbours_ref, counts_ref, block_ref, out_ref, held, blank, in_sem, out_sem):
    here = lax.axis_index("row") * lax.axis_size("col") + lax.axis_index("col")
    halves, wide = block_ref.shape[1], block_ref.shape[3]
    blank[...] = jnp.zeros_like(blank)

    def fetch(j, h):
        at = jnp.clip(neighbours_ref[0, j] - here + (W - 1), 0, 2 * W - 2)
        return pltpu.make_async_copy(block_ref.at[at, h], held.at[j, :, pl.ds(h * wide, wide)], in_sem.at[j, h])

    def store(j, source):
        return pltpu.make_async_copy(source, out_ref.at[j], out_sem.at[j])

    slots = out_ref.shape[0]
    for j in range(slots):

        @pl.when(j < counts_ref[0])
        def _():
            for h in range(halves):
                fetch(j, h).start()

        @pl.when(j >= counts_ref[0])
        def _():
            store(j, blank).start()

    for j in range(slots):

        @pl.when(j < counts_ref[0])
        def _():
            for h in range(halves):
                fetch(j, h).wait()
            store(j, held.at[j]).start()

    for j in range(slots):
        store(j, blank).wait()


def shards(coeffs, occupations, block_order, neighbours, counts):
    rows, cols = lax.axis_size("row"), lax.axis_size("col")
    states = coeffs.shape[1]
    depth = coeffs.shape[0] // cols
    per = -(-W // cols)
    size = per * cols
    units, half = cols * HALVES, depth // HALVES
    slots_total = 2 * W - 1
    own = coeffs.reshape(cols, depth, states)
    occ = occupations.reshape(cols, 1, states)
    dma = pltpu.SemaphoreType.DMA
    blocks = pl.pallas_call(
        functools.partial(kernel, rows, cols, per),
        out_shape=jax.ShapeDtypeStruct((slots_total, HALVES, depth, half), jnp.bfloat16),
        in_specs=[
            pl.BlockSpec(memory_space=pl.ANY),
            pl.BlockSpec(memory_space=pltpu.SMEM),
            pl.BlockSpec(memory_space=pltpu.VMEM),
        ],
        out_specs=pl.BlockSpec(memory_space=pl.ANY),
        scratch_shapes=[
            pltpu.VMEM((cols, depth, states), jnp.bfloat16),
            pltpu.VMEM((per, units, cols, half, states), jnp.bfloat16),
            pltpu.VMEM((2, HALVES, cols, half, states), jnp.bfloat16),
            pltpu.VMEM((3, cols, depth, states), jnp.bfloat16),
            pltpu.VMEM((2 * size - 1, HALVES, depth, half), jnp.bfloat16),
            dma,
            dma((2, units, cols)),
            dma((max(per - 1, 1), units, cols)),
            dma((per, units, cols)),
            dma((2, HALVES, cols)),
            dma((HALVES, cols)),
            dma((2, HALVES, cols)),
            dma((2 * size - 1, HALVES)),
            dma((slots_total, HALVES)),
        ],
        compiler_params=pltpu.CompilerParams(
            collective_id=0, has_side_effects=True, vmem_limit_bytes=60 * 1024 * 1024
        ),
        name="density_blocks",
    )(own, block_order, occ)
    slots = neighbours.shape[1]
    placed = pl.pallas_call(
        place_blocks,
        out_shape=jax.ShapeDtypeStruct((slots, depth, depth), jnp.bfloat16),
        in_specs=[
            pl.BlockSpec(memory_space=pltpu.SMEM),
            pl.BlockSpec(memory_space=pltpu.SMEM),
            pl.BlockSpec(memory_space=pl.ANY),
        ],
        out_specs=pl.BlockSpec(memory_space=pl.ANY),
        scratch_shapes=[
            pltpu.VMEM((slots, depth, depth), jnp.bfloat16),
            pltpu.VMEM((depth, depth), jnp.bfloat16),
            dma((slots, HALVES)),
            dma((slots,)),
        ],
        name="place_blocks",
    )(neighbours, counts, blocks)
    return placed[None]


def solution(mesh):
    return jax.shard_map(
        shards,
        mesh=mesh,
        in_specs=(P("row", "col"), P(), P(), P(("row", "col"), None), P(("row", "col"))),
        out_specs=P(("row", "col"), None, None, None),
        check_vma=False,
    )
```

```python
import functools

import jax
import jax.numpy as jnp
from jax import lax
from jax.experimental import pallas as pl
from jax.experimental.pallas import tpu as pltpu
from jax.sharding import PartitionSpec as P

W = 8
HALVES = 2
MESH = pl.DeviceIdType.MESH


def kernel(rows, cols, per, own_ref, order_ref, occ_ref, out_ref, stage, gat, raw, wgt, res, in_sem, fsem, psem, rsem, xsem, ysem, usem, osem, qsem):
    row, z = lax.axis_index("row"), lax.axis_index("col")
    k = lax.rem(row, per)
    base = row - k
    place = k * cols + z
    size = per * cols
    halves = raw.shape[1]
    units = cols * halves
    mid = cols // 2
    has_up, has_down = row + per < rows, row >= per
    has_up2, has_down2 = row + 2 * per < rows, row >= 2 * per
    odd = lax.rem(row // per, 2) == 1
    ships_up = has_up & jnp.logical_not(odd) & ((place > 0) | has_down)
    ships_down = has_down & jnp.where(odd, (place < size - 1) | has_up, (place < size - 1) & jnp.logical_not(has_up))
    relays_up = has_up2 & (place > 0) & jnp.logical_not(odd)
    relays_down = has_down2 & (place < size - 1) & odd
    lower, upper = has_down & (place > 0), has_up & (place < size - 1)
    own_done = (jnp.minimum(z, cols - 1 - z) + 1) * halves - 1
    direct = (odd, jnp.logical_not(odd) | jnp.logical_not(has_up2))
    away_step = [jnp.minimum(jnp.where(d, own_done + 1, own_done + 2), units - 1) for d in direct]

    def remote(src, dst, send, recv, device):
        return pltpu.make_async_remote_copy(
            src_ref=src, dst_ref=dst, send_sem=send, recv_sem=recv, device_id=device, device_id_type=MESH
        )

    def onward(way, v, c):
        there = lax.rem(z + 1 - 2 * way + cols, cols)
        return remote(gat.at[k, v, c], gat.at[k, v, c], fsem.at[way, v, c], rsem.at[k, v, c], (row, there))

    def partner(d, v, c):
        there = base + lax.rem(k + d, per)
        return remote(gat.at[k, v, c], gat.at[k, v, c], psem.at[d - 1, v, c], rsem.at[k, v, c], (there, z))

    def ship(way, h, c):
        there = lax.rem(row + (1 - 2 * way) * per + rows, rows)
        return remote(gat.at[k, z * halves + h, c], raw.at[way, h, c], xsem.at[way, h, c], usem.at[way, h, c], (there, z))

    def relay(way, h, c):
        there = lax.rem(row + (2 - 4 * way) * per + 2 * rows, rows)
        return remote(raw.at[1 - way, h, c], raw.at[way, h, c], ysem.at[h, c], usem.at[way, h, c], (there, z))

    def taken(way, h, c):
        remote(raw.at[way, h, c], raw.at[way, h, c], xsem.at[0, 0, 0], usem.at[way, h, c], (row, z)).wait_recv()

    def arrive(kk, v, c):
        remote(gat.at[kk, v, c], gat.at[kk, v, c], fsem.at[0, 0, 0], rsem.at[kk, v, c], (row, z)).wait_recv()

    def ship_on(h, c, act):
        @pl.when(ships_up)
        def _():
            act(ship(0, h, c))

        @pl.when(ships_down)
        def _():
            act(ship(1, h, c))

    def start(copy):
        copy.start()

    def sent(copy):
        copy.wait_send()

    fill = pltpu.make_async_copy(own_ref, stage, in_sem)
    fill.start()
    barrier = pltpu.get_barrier_semaphore()
    for d in range(1, per):
        pl.semaphore_signal(barrier, inc=1, device_id=(base + lax.rem(k + d, per), z), device_id_type=MESH)

    greeted = per - 1
    for present, step in ((z < cols - 1, 1), (z > 0, -1)):
        greeted = greeted + present.astype(jnp.int32)

        @pl.when(present)
        def _():
            pl.semaphore_signal(barrier, inc=1, device_id=(row, lax.rem(z + step + cols, cols)), device_id_type=MESH)

    for present, step in ((has_up, per), (has_down, -per), (has_up2, 2 * per), (has_down2, -2 * per)):
        greeted = greeted + present.astype(jnp.int32)

        @pl.when(present)
        def _():
            there = lax.rem(row + step + 2 * rows, rows)
            pl.semaphore_signal(barrier, inc=1, device_id=(there, z), device_id_type=MESH)

    fill.wait()

    first = row * cols

    @pl.loop(0, cols)
    def _(i):
        pick = jnp.clip(order_ref[first + i] - first, 0, cols - 1)

        @pl.loop(0, halves)
        def _(h):
            rows_of = stage.shape[1] // halves
            gat[k, i * halves + h, z] = stage[pick, pl.ds(pl.multiple_of(h * rows_of, rows_of), rows_of)]

    pl.semaphore_wait(barrier, greeted)

    def early(n):
        return 2 * n < units - 1

    def due(way, v, n):
        if way == 0:
            return (z < cols - 1) & jnp.where(z + 1 >= mid, v == units - 1 - n, early(n))
        return (z > 0) & jnp.where(z - 1 < mid, v == n, early(n))

    def awaited(way, v, n):
        if way == 0:
            return jnp.where(z >= mid, v == units - 1 - n, early(n))
        return jnp.where(z < mid, v == n, early(n))

    def own_sends(way, m):
        for v in (units - 1 - m, m) if way == 0 else (m, units - 1 - m):

            @pl.when(due(way, v, m))
            def _():
                onward(way, v, z).start()

    ahead = (jnp.where(z == 0, units, z), jnp.where(z == cols - 1, units, cols - 1 - z))
    for way in (0, 1):

        @pl.loop(0, jnp.minimum(ahead[way], units))
        def _(m):
            own_sends(way, m)

    @pl.loop(0, halves)
    def _(h):
        ship_on(h, z, start)

    @pl.loop(0, units)
    def _(v):
        for d in range(1, per):
            partner(d, v, z).start()

    def got(v, c):
        arrive(k, v, c)
        for d in range(1, per):
            partner(d, v, c).start()

        @pl.when(v // halves == z)
        def _():
            ship_on(lax.rem(v, halves), c, start)

    def gather(n):
        for way in (0, 1):

            @pl.when(n + ahead[way] < units)
            def _():
                own_sends(way, n + ahead[way])

        @pl.loop(1, cols)
        def _(s):
            for way, v in ((0, units - 1 - n), (1, n), (0, n), (1, units - 1 - n)):
                c = z - s if way == 0 else z + s
                there = c >= 0 if way == 0 else c < cols

                @pl.when(there & awaited(way, v, n))
                def _():
                    got(v, c)

                @pl.when(there & due(way, v, n))
                def _():
                    onward(way, v, c).start()

    def relay_on(h, c, act):
        @pl.when(relays_up)
        def _():
            act(relay(0, h, c), 1)

        @pl.when(relays_down)
        def _():
            act(relay(1, h, c), 0)

    def receive_and_relay(h, c):
        def act(copy, way):
            taken(way, h, c)
            copy.start()

        relay_on(h, c, act)

    def ship_step(h, c):
        v = z * halves + h
        middle = jnp.minimum(v, units - 1 - v)
        below = jnp.where(z >= mid, units - 1 - v, middle)
        above = jnp.where(z < mid, v, middle)
        return jnp.where(c == z, 0, jnp.where(c < z, below, above))

    def relay_due(n):
        def maybe(h, c):
            @pl.when((c >= 0) & (c < cols) & (ship_step(h, c) == n))
            def _():
                receive_and_relay(h, c)

        @pl.loop(0, halves)
        def _(h):
            maybe(h, z)

            @pl.loop(1, cols)
            def _(s):
                maybe(h, z - s)
                maybe(h, z + s)

    def scale(way, source):
        rows_of = wgt.shape[2] // halves
        for h in range(halves):

            @pl.loop(0, cols)
            def _(c):
                wgt[way, c, h * rows_of : (h + 1) * rows_of] = (source(h, c).astype(jnp.float32) * occ_ref[c]).astype(jnp.bfloat16)

    def prepare_away(way):
        present, waited = ((lower, relays_down), (upper, relays_up))[way]

        @pl.when(present)
        def _():
            @pl.when(jnp.logical_not(waited))
            def _():
                @pl.loop(0, halves)
                def _(h):
                    @pl.loop(0, cols)
                    def _(c):
                        taken(way, h, c)

            scale(way, lambda h, c: raw[way, h, c])

    def prepare_home():
        scale(2, lambda h, c: gat[k, z * halves + h, c])

    def answer(t):
        low = t < place
        other = jnp.where(low, t, t + 1)
        slot = jnp.where(low, size + other - place, other - place - size) + W - 1
        near = (slot >= 0) & (slot < 2 * W - 1)
        return low, other, slot, near

    def reply(t, h):
        low, other, slot, near = answer(t)
        there = lax.rem(jnp.where(low, row - per, row + per) + rows, rows)
        go = near & jnp.where(low, row - per >= 0, row + per < rows)
        slot = jnp.clip(slot, 0, 2 * W - 2)
        return go, remote(res.at[t, h], out_ref.at[slot, h], osem.at[t, h], qsem.at[slot, h], (there, z))

    def local(t, h):
        other = t - (size - 1)
        slot = other - place + W - 1
        near = (slot >= 0) & (slot < 2 * W - 1)
        slot = jnp.clip(slot, 0, 2 * W - 2)
        return near, pltpu.make_async_copy(res.at[t, h], out_ref.at[slot, h], osem.at[t, h])

    def product(t, way, kk, v):
        total = jnp.zeros(res.shape[2:], jnp.float32)
        for c in range(cols):
            total = total + lax.dot_general(
                wgt[way, c], gat[kk, v, c], (((1,), (1,)), ((), ())), preferred_element_type=jnp.float32
            )
        res[t, lax.rem(v, halves)] = total.astype(jnp.bfloat16)

    def home(kk, v):
        t = kk * cols + v // halves + size - 1
        near, copy = local(t, lax.rem(v, halves))

        @pl.when(near)
        def _():
            product(t, 2, kk, v)
            copy.start()

    def away(way, kk, v):
        other = kk * cols + v // halves
        t = jnp.clip(other - way, 0, size - 2)
        go, copy = reply(t, lax.rem(v, halves))

        @pl.when(go & ((other < place) if way == 0 else (other > place)))
        def _():
            product(t, way, kk, v)
            copy.start()

    def unit(n):
        return jnp.where(z < mid, n, units - 1 - n)

    def work(n, since, prepare, each):
        @pl.when(n == since)
        def _():
            prepare()

        @pl.when(n >= since)
        def _():
            @pl.loop(jnp.where(n == since, 0, n), n + 1)
            def _(m):
                @pl.loop(0, per)
                def _(kk):
                    each(kk, unit(m))

    @pl.loop(0, units)
    def _(n):
        gather(n)
        for d in range(1, per):
            kk = lax.rem(k + d, per)

            @pl.loop(0, cols)
            def _(c):
                arrive(kk, unit(n), c)

        for way in (0, 1):
            work(n, away_step[way], functools.partial(prepare_away, way), functools.partial(away, way))
        work(n, own_done, prepare_home, home)
        relay_due(n)

    @pl.loop(0, units)
    def _(v):
        @pl.loop(0, cols)
        def _(c):
            @pl.when((z < cols - 1) & (c <= z))
            def _():
                onward(0, v, c).wait_send()

            @pl.when((z > 0) & (c >= z))
            def _():
                onward(1, v, c).wait_send()

            for d in range(1, per):
                partner(d, v, c).wait_send()

    @pl.loop(0, halves)
    def _(h):
        @pl.loop(0, cols)
        def _(c):
            ship_on(h, c, sent)
            relay_on(h, c, lambda copy, way: sent(copy))

        @pl.loop(0, size - 1)
        def _(t):
            go, copy = reply(t, h)

            @pl.when(go)
            def _():
                copy.wait_send()

            low, other, slot, near = answer(t)
            arrives = near & jnp.where(low, row + per < rows, row - per >= 0)
            slot = jnp.clip(slot, 0, 2 * W - 2)

            @pl.when(arrives)
            def _():
                remote(res.at[t, h], out_ref.at[slot, h], osem.at[t, h], qsem.at[slot, h], (row, z)).wait_recv()

        @pl.loop(size - 1, 2 * size - 1)
        def _(t):
            near, copy = local(t, h)

            @pl.when(near)
            def _():
                copy.wait()


def place_blocks(neighbours_ref, counts_ref, block_ref, out_ref, held, blank, in_sem, out_sem):
    here = lax.axis_index("row") * lax.axis_size("col") + lax.axis_index("col")
    halves, wide = block_ref.shape[1], block_ref.shape[3]
    blank[...] = jnp.zeros_like(blank)

    def fetch(j, h):
        at = jnp.clip(neighbours_ref[0, j] - here + (W - 1), 0, 2 * W - 2)
        return pltpu.make_async_copy(block_ref.at[at, h], held.at[j, :, pl.ds(h * wide, wide)], in_sem.at[j, h])

    def store(j, source):
        return pltpu.make_async_copy(source, out_ref.at[j], out_sem.at[j])

    slots = out_ref.shape[0]
    for j in range(slots):

        @pl.when(j < counts_ref[0])
        def _():
            for h in range(halves):
                fetch(j, h).start()

        @pl.when(j >= counts_ref[0])
        def _():
            store(j, blank).start()

    for j in range(slots):

        @pl.when(j < counts_ref[0])
        def _():
            for h in range(halves):
                fetch(j, h).wait()
            store(j, held.at[j]).start()

    for j in range(slots):
        store(j, blank).wait()


def shards(coeffs, occupations, block_order, neighbours, counts):
    rows, cols = lax.axis_size("row"), lax.axis_size("col")
    states = coeffs.shape[1]
    depth = coeffs.shape[0] // cols
    per = -(-W // cols)
    size = per * cols
    units, half = cols * HALVES, depth // HALVES
    slots_total = 2 * W - 1
    own = coeffs.reshape(cols, depth, states)
    occ = occupations.reshape(cols, 1, states)
    dma = pltpu.SemaphoreType.DMA
    blocks = pl.pallas_call(
        functools.partial(kernel, rows, cols, per),
        out_shape=jax.ShapeDtypeStruct((slots_total, HALVES, depth, half), jnp.bfloat16),
        in_specs=[
            pl.BlockSpec(memory_space=pl.ANY),
            pl.BlockSpec(memory_space=pltpu.SMEM),
            pl.BlockSpec(memory_space=pltpu.VMEM),
        ],
        out_specs=pl.BlockSpec(memory_space=pl.ANY),
        scratch_shapes=[
            pltpu.VMEM((cols, depth, states), jnp.bfloat16),
            pltpu.VMEM((per, units, cols, half, states), jnp.bfloat16),
            pltpu.VMEM((2, HALVES, cols, half, states), jnp.bfloat16),
            pltpu.VMEM((3, cols, depth, states), jnp.bfloat16),
            pltpu.VMEM((2 * size - 1, HALVES, depth, half), jnp.bfloat16),
            dma,
            dma((2, units, cols)),
            dma((max(per - 1, 1), units, cols)),
            dma((per, units, cols)),
            dma((2, HALVES, cols)),
            dma((HALVES, cols)),
            dma((2, HALVES, cols)),
            dma((2 * size - 1, HALVES)),
            dma((slots_total, HALVES)),
        ],
        compiler_params=pltpu.CompilerParams(
            collective_id=0, has_side_effects=True, vmem_limit_bytes=60 * 1024 * 1024
        ),
        name="density_blocks",
    )(own, block_order, occ)
    slots = neighbours.shape[1]
    placed = pl.pallas_call(
        place_blocks,
        out_shape=jax.ShapeDtypeStruct((slots, depth, depth), jnp.bfloat16),
        in_specs=[
            pl.BlockSpec(memory_space=pltpu.SMEM),
            pl.BlockSpec(memory_space=pltpu.SMEM),
            pl.BlockSpec(memory_space=pl.ANY),
        ],
        out_specs=pl.BlockSpec(memory_space=pl.ANY),
        scratch_shapes=[
            pltpu.VMEM((slots, depth, depth), jnp.bfloat16),
            pltpu.VMEM((depth, depth), jnp.bfloat16),
            dma((slots, HALVES)),
            dma((slots,)),
        ],
        name="place_blocks",
    )(neighbours, counts, blocks)
    return placed[None]


def solution(mesh):
    return jax.shard_map(
        shards,
        mesh=mesh,
        in_specs=(P("row", "col"), P(), P(), P(("row", "col"), None), P(("row", "col"))),
        out_specs=P(("row", "col"), None, None, None),
        check_vma=False,
    )
```

```python
import functools

import jax
import jax.numpy as jnp
from jax import lax
from jax.experimental import pallas as pl
from jax.experimental.pallas import tpu as pltpu
from jax.sharding import PartitionSpec as P

W = 8
HALVES = 2
MESH = pl.DeviceIdType.MESH


def kernel(rows, cols, per, own_ref, order_ref, occ_ref, out_ref, stage, gat, raw, wgt, res, hop, in_sem, fsem, psem, rsem, xsem, ysem, usem, osem, qsem, hsem, ssem):
    row, z = lax.axis_index("row"), lax.axis_index("col")
    k = lax.rem(row, per)
    base = row - k
    place = k * cols + z
    size = per * cols
    halves = raw.shape[1]
    units = cols * halves
    mid = cols // 2
    has_up, has_down = row + per < rows, row >= per
    has_up2, has_down2 = row + 2 * per < rows, row >= 2 * per
    odd = lax.rem(row // per, 2) == 1
    ships_up = has_up & jnp.logical_not(odd) & ((place > 0) | has_down)
    ships_down = has_down & jnp.where(odd, (place < size - 1) | has_up, (place < size - 1) & jnp.logical_not(has_up))
    relays_up = has_up2 & (place > 0) & jnp.logical_not(odd)
    relays_down = has_down2 & (place < size - 1) & odd
    lower, upper = has_down & (place > 0), has_up & (place < size - 1)
    own_done = (jnp.minimum(z, cols - 1 - z) + 1) * halves - 1
    direct = (odd, jnp.logical_not(odd) | jnp.logical_not(has_up2))
    bends = (jnp.logical_not(odd) & has_down2, odd & has_up2)
    carries = (jnp.logical_not(odd) & has_up2, odd & has_down2)
    bend_step = jnp.minimum(own_done + 2, units - 1)
    away_step = [jnp.minimum(jnp.where(d, own_done + 1, own_done + 2), units - 1) for d in direct]

    def remote(src, dst, send, recv, device):
        return pltpu.make_async_remote_copy(
            src_ref=src, dst_ref=dst, send_sem=send, recv_sem=recv, device_id=device, device_id_type=MESH
        )

    def onward(way, v, c):
        there = lax.rem(z + 1 - 2 * way + cols, cols)
        return remote(gat.at[k, v, c], gat.at[k, v, c], fsem.at[way, v, c], rsem.at[k, v, c], (row, there))

    def partner(d, v, c):
        there = base + lax.rem(k + d, per)
        return remote(gat.at[k, v, c], gat.at[k, v, c], psem.at[d - 1, v, c], rsem.at[k, v, c], (there, z))

    def ship(way, h, c):
        there = lax.rem(row + (1 - 2 * way) * per + rows, rows)
        return remote(gat.at[k, z * halves + h, c], raw.at[way, h, c], xsem.at[way, h, c], usem.at[way, h, c], (there, z))

    def relay(way, h, c):
        there = lax.rem(row + (2 - 4 * way) * per + 2 * rows, rows)
        return remote(raw.at[1 - way, h, c], raw.at[way, h, c], ysem.at[h, c], usem.at[way, h, c], (there, z))

    def taken(way, h, c):
        remote(raw.at[way, h, c], raw.at[way, h, c], xsem.at[0, 0, 0], usem.at[way, h, c], (row, z)).wait_recv()

    def arrive(kk, v, c):
        remote(gat.at[kk, v, c], gat.at[kk, v, c], fsem.at[0, 0, 0], rsem.at[kk, v, c], (row, z)).wait_recv()

    def ship_on(h, c, act):
        @pl.when(ships_up)
        def _():
            act(ship(0, h, c))

        @pl.when(ships_down)
        def _():
            act(ship(1, h, c))

    def start(copy):
        copy.start()

    def sent(copy):
        copy.wait_send()

    fill = pltpu.make_async_copy(own_ref, stage, in_sem)
    fill.start()
    barrier = pltpu.get_barrier_semaphore()
    for d in range(1, per):
        pl.semaphore_signal(barrier, inc=1, device_id=(base + lax.rem(k + d, per), z), device_id_type=MESH)

    greeted = per - 1
    for present, step in ((z < cols - 1, 1), (z > 0, -1)):
        greeted = greeted + present.astype(jnp.int32)

        @pl.when(present)
        def _():
            pl.semaphore_signal(barrier, inc=1, device_id=(row, lax.rem(z + step + cols, cols)), device_id_type=MESH)

    for present, step in ((has_up, per), (has_down, -per), (has_up2, 2 * per), (has_down2, -2 * per)):
        greeted = greeted + present.astype(jnp.int32)

        @pl.when(present)
        def _():
            there = lax.rem(row + step + 2 * rows, rows)
            pl.semaphore_signal(barrier, inc=1, device_id=(there, z), device_id_type=MESH)

    fill.wait()

    first = row * cols

    @pl.loop(0, cols)
    def _(i):
        pick = jnp.clip(order_ref[first + i] - first, 0, cols - 1)

        @pl.loop(0, halves)
        def _(h):
            rows_of = stage.shape[1] // halves
            gat[k, i * halves + h, z] = stage[pick, pl.ds(pl.multiple_of(h * rows_of, rows_of), rows_of)]

    pl.semaphore_wait(barrier, greeted)

    def early(n):
        return 2 * n < units - 1

    def due(way, v, n):
        if way == 0:
            return (z < cols - 1) & jnp.where(z + 1 >= mid, v == units - 1 - n, early(n))
        return (z > 0) & jnp.where(z - 1 < mid, v == n, early(n))

    def awaited(way, v, n):
        if way == 0:
            return jnp.where(z >= mid, v == units - 1 - n, early(n))
        return jnp.where(z < mid, v == n, early(n))

    def own_sends(way, m):
        for v in (units - 1 - m, m) if way == 0 else (m, units - 1 - m):

            @pl.when(due(way, v, m))
            def _():
                onward(way, v, z).start()

    ahead = (jnp.where(z == 0, units, z), jnp.where(z == cols - 1, units, cols - 1 - z))
    for way in (0, 1):

        @pl.loop(0, jnp.minimum(ahead[way], units))
        def _(m):
            own_sends(way, m)

    @pl.loop(0, halves)
    def _(h):
        ship_on(h, z, start)

    @pl.loop(0, units)
    def _(v):
        for d in range(1, per):
            partner(d, v, z).start()

    def got(v, c):
        arrive(k, v, c)
        for d in range(1, per):
            partner(d, v, c).start()

        @pl.when(v // halves == z)
        def _():
            ship_on(lax.rem(v, halves), c, start)

    def gather(n):
        for way in (0, 1):

            @pl.when(n + ahead[way] < units)
            def _():
                own_sends(way, n + ahead[way])

        @pl.loop(1, cols)
        def _(s):
            for way, v in ((0, units - 1 - n), (1, n), (0, n), (1, units - 1 - n)):
                c = z - s if way == 0 else z + s
                there = c >= 0 if way == 0 else c < cols

                @pl.when(there & awaited(way, v, n))
                def _():
                    got(v, c)

                @pl.when(there & due(way, v, n))
                def _():
                    onward(way, v, c).start()

    def relay_on(h, c, act):
        @pl.when(relays_up)
        def _():
            act(relay(0, h, c), 1)

        @pl.when(relays_down)
        def _():
            act(relay(1, h, c), 0)

    def receive_and_relay(h, c):
        def act(copy, way):
            taken(way, h, c)
            copy.start()

        relay_on(h, c, act)

    def ship_step(h, c):
        v = z * halves + h
        middle = jnp.minimum(v, units - 1 - v)
        below = jnp.where(z >= mid, units - 1 - v, middle)
        above = jnp.where(z < mid, v, middle)
        return jnp.where(c == z, 0, jnp.where(c < z, below, above))

    def relay_due(n):
        def maybe(h, c):
            @pl.when((c >= 0) & (c < cols) & (ship_step(h, c) == n))
            def _():
                receive_and_relay(h, c)

        @pl.loop(0, halves)
        def _(h):
            maybe(h, z)

            @pl.loop(1, cols)
            def _(s):
                maybe(h, z - s)
                maybe(h, z + s)

    def scale(way, source):
        rows_of = wgt.shape[2] // halves
        for h in range(halves):

            @pl.loop(0, cols)
            def _(c):
                wgt[way, c, h * rows_of : (h + 1) * rows_of] = (source(h, c).astype(jnp.float32) * occ_ref[c]).astype(jnp.bfloat16)

    def prepare_away(way):
        present, waited = ((lower, relays_down), (upper, relays_up))[way]

        @pl.when(present)
        def _():
            @pl.when(jnp.logical_not(waited))
            def _():
                @pl.loop(0, halves)
                def _(h):
                    @pl.loop(0, cols)
                    def _(c):
                        taken(way, h, c)

            scale(way, lambda h, c: raw[way, h, c])

    def prepare_home():
        scale(2, lambda h, c: gat[k, z * halves + h, c])

    def answer(t):
        low = t < place
        other = jnp.where(low, t, t + 1)
        slot = jnp.where(low, size + other - place, other - place - size) + W - 1
        near = (slot >= 0) & (slot < 2 * W - 1)
        return low, other, slot, near

    def reply(t, h):
        low, other, slot, near = answer(t)
        there = lax.rem(jnp.where(low, row - per, row + per) + rows, rows)
        go = near & jnp.where(low, row - per >= 0, row + per < rows)
        slot = jnp.clip(slot, 0, 2 * W - 2)
        return go, remote(res.at[t, h], out_ref.at[slot, h], osem.at[t, h], qsem.at[slot, h], (there, z))

    def bend(way, t, h):
        there = lax.rem(row + (4 * way - 2) * per + 2 * rows, rows)
        return remote(res.at[t, h], hop.at[t, h], osem.at[t, h], hsem.at[t, h], (there, z))

    def carry(way, t, h):
        low, other, slot, near = answer(t)
        there = lax.rem(row + (1 - 2 * way) * per + rows, rows)
        slot = jnp.clip(slot, 0, 2 * W - 2)
        go = carries[way] & near & (low if way == 0 else jnp.logical_not(low))
        return go, remote(hop.at[t, h], out_ref.at[slot, h], ssem.at[t, h], qsem.at[slot, h], (there, z))

    def bent(m):
        return lax.rem(m, 2) == 0

    def unit(n):
        return jnp.where(z < mid, n, units - 1 - n)

    def local(t, h):
        other = t - (size - 1)
        slot = other - place + W - 1
        near = (slot >= 0) & (slot < 2 * W - 1)
        slot = jnp.clip(slot, 0, 2 * W - 2)
        return near, pltpu.make_async_copy(res.at[t, h], out_ref.at[slot, h], osem.at[t, h])

    def product(t, way, kk, v):
        total = jnp.zeros(res.shape[2:], jnp.float32)
        for c in range(cols):
            total = total + lax.dot_general(
                wgt[way, c], gat[kk, v, c], (((1,), (1,)), ((), ())), preferred_element_type=jnp.float32
            )
        res[t, lax.rem(v, halves)] = total.astype(jnp.bfloat16)

    def home(kk, m):
        v = unit(m)
        t = kk * cols + v // halves + size - 1
        near, copy = local(t, lax.rem(v, halves))

        @pl.when(near)
        def _():
            product(t, 2, kk, v)
            copy.start()

    def away(way, kk, m):
        v = unit(m)
        other = kk * cols + v // halves
        t = jnp.clip(other - way, 0, size - 2)
        go, copy = reply(t, lax.rem(v, halves))

        @pl.when(go & ((other < place) if way == 0 else (other > place)))
        def _():
            product(t, way, kk, v)
            bends_now = bends[way] & bent(m)

            @pl.when(bends_now)
            def _():
                bend(way, t, lax.rem(v, halves)).start()

            @pl.when(jnp.logical_not(bends_now))
            def _():
                copy.start()

    def carry_due(n):
        def one(m):
            v = unit(m)
            h = lax.rem(v, halves)
            for way in (0, 1):

                @pl.loop(0, per)
                def _(kk):
                    other = kk * cols + v // halves
                    t = jnp.clip(other - way, 0, size - 2)
                    go, copy = carry(way, t, h)

                    @pl.when(go & ((other < place) if way == 0 else (other > place)) & bent(m))
                    def _():
                        remote(hop.at[t, h], hop.at[t, h], ssem.at[0, 0], hsem.at[t, h], (row, z)).wait_recv()
                        copy.start()

        @pl.when(n > bend_step)
        def _():
            @pl.loop(jnp.where(n == bend_step + 1, 0, n - 1), n)
            def _(m):
                one(m)

    def work(n, since, prepare, each):
        @pl.when(n == since)
        def _():
            prepare()

        @pl.when(n >= since)
        def _():
            @pl.loop(jnp.where(n == since, 0, n), n + 1)
            def _(m):
                @pl.loop(0, per)
                def _(kk):
                    each(kk, m)

    @pl.loop(0, units)
    def _(n):
        gather(n)
        for d in range(1, per):
            kk = lax.rem(k + d, per)

            @pl.loop(0, cols)
            def _(c):
                arrive(kk, unit(n), c)

        for way in (0, 1):
            work(n, away_step[way], functools.partial(prepare_away, way), functools.partial(away, way))
        work(n, own_done, prepare_home, home)
        relay_due(n)
        carry_due(n)

    carry_due(units)

    @pl.loop(0, units)
    def _(v):
        @pl.loop(0, cols)
        def _(c):
            @pl.when((z < cols - 1) & (c <= z))
            def _():
                onward(0, v, c).wait_send()

            @pl.when((z > 0) & (c >= z))
            def _():
                onward(1, v, c).wait_send()

            for d in range(1, per):
                partner(d, v, c).wait_send()

    @pl.loop(0, halves)
    def _(h):
        @pl.loop(0, cols)
        def _(c):
            ship_on(h, c, sent)
            relay_on(h, c, lambda copy, way: sent(copy))

        @pl.loop(0, size - 1)
        def _(t):
            go, copy = reply(t, h)

            @pl.when(go)
            def _():
                copy.wait_send()

            for way in (0, 1):
                go, copy = carry(way, t, h)

                @pl.when(go & bent(unit((t + way) % cols * halves + h)))
                def _():
                    copy.wait_send()

            low, other, slot, near = answer(t)
            arrives = near & jnp.where(low, row + per < rows, row - per >= 0)
            slot = jnp.clip(slot, 0, 2 * W - 2)

            @pl.when(arrives)
            def _():
                remote(res.at[t, h], out_ref.at[slot, h], osem.at[t, h], qsem.at[slot, h], (row, z)).wait_recv()

        @pl.loop(size - 1, 2 * size - 1)
        def _(t):
            near, copy = local(t, h)

            @pl.when(near)
            def _():
                copy.wait()


def place_blocks(neighbours_ref, counts_ref, block_ref, out_ref, held, blank, in_sem, out_sem):
    here = lax.axis_index("row") * lax.axis_size("col") + lax.axis_index("col")
    halves, wide = block_ref.shape[1], block_ref.shape[3]
    blank[...] = jnp.zeros_like(blank)

    def fetch(j, h):
        at = jnp.clip(neighbours_ref[0, j] - here + (W - 1), 0, 2 * W - 2)
        return pltpu.make_async_copy(block_ref.at[at, h], held.at[j, :, pl.ds(h * wide, wide)], in_sem.at[j, h])

    def store(j, source):
        return pltpu.make_async_copy(source, out_ref.at[j], out_sem.at[j])

    slots = out_ref.shape[0]
    for j in range(slots):

        @pl.when(j < counts_ref[0])
        def _():
            for h in range(halves):
                fetch(j, h).start()

        @pl.when(j >= counts_ref[0])
        def _():
            store(j, blank).start()

    for j in range(slots):

        @pl.when(j < counts_ref[0])
        def _():
            for h in range(halves):
                fetch(j, h).wait()
            store(j, held.at[j]).start()

    for j in range(slots):
        store(j, blank).wait()


def shards(coeffs, occupations, block_order, neighbours, counts):
    rows, cols = lax.axis_size("row"), lax.axis_size("col")
    states = coeffs.shape[1]
    depth = coeffs.shape[0] // cols
    per = -(-W // cols)
    size = per * cols
    units, half = cols * HALVES, depth // HALVES
    slots_total = 2 * W - 1
    own = coeffs.reshape(cols, depth, states)
    occ = occupations.reshape(cols, 1, states)
    dma = pltpu.SemaphoreType.DMA
    blocks = pl.pallas_call(
        functools.partial(kernel, rows, cols, per),
        out_shape=jax.ShapeDtypeStruct((slots_total, HALVES, depth, half), jnp.bfloat16),
        in_specs=[
            pl.BlockSpec(memory_space=pl.ANY),
            pl.BlockSpec(memory_space=pltpu.SMEM),
            pl.BlockSpec(memory_space=pltpu.VMEM),
        ],
        out_specs=pl.BlockSpec(memory_space=pl.ANY),
        scratch_shapes=[
            pltpu.VMEM((cols, depth, states), jnp.bfloat16),
            pltpu.VMEM((per, units, cols, half, states), jnp.bfloat16),
            pltpu.VMEM((2, HALVES, cols, half, states), jnp.bfloat16),
            pltpu.VMEM((3, cols, depth, states), jnp.bfloat16),
            pltpu.VMEM((2 * size - 1, HALVES, depth, half), jnp.bfloat16),
            pltpu.VMEM((size - 1, HALVES, depth, half), jnp.bfloat16),
            dma,
            dma((2, units, cols)),
            dma((max(per - 1, 1), units, cols)),
            dma((per, units, cols)),
            dma((2, HALVES, cols)),
            dma((HALVES, cols)),
            dma((2, HALVES, cols)),
            dma((2 * size - 1, HALVES)),
            dma((slots_total, HALVES)),
            dma((size - 1, HALVES)),
            dma((size - 1, HALVES)),
        ],
        compiler_params=pltpu.CompilerParams(
            collective_id=0, has_side_effects=True, vmem_limit_bytes=60 * 1024 * 1024
        ),
        name="density_blocks",
    )(own, block_order, occ)
    slots = neighbours.shape[1]
    placed = pl.pallas_call(
        place_blocks,
        out_shape=jax.ShapeDtypeStruct((slots, depth, depth), jnp.bfloat16),
        in_specs=[
            pl.BlockSpec(memory_space=pltpu.SMEM),
            pl.BlockSpec(memory_space=pltpu.SMEM),
            pl.BlockSpec(memory_space=pl.ANY),
        ],
        out_specs=pl.BlockSpec(memory_space=pl.ANY),
        scratch_shapes=[
            pltpu.VMEM((slots, depth, depth), jnp.bfloat16),
            pltpu.VMEM((depth, depth), jnp.bfloat16),
            dma((slots, HALVES)),
            dma((slots,)),
        ],
        name="place_blocks",
    )(neighbours, counts, blocks)
    return placed[None]


def solution(mesh):
    return jax.shard_map(
        shards,
        mesh=mesh,
        in_specs=(P("row", "col"), P(), P(), P(("row", "col"), None), P(("row", "col"))),
        out_specs=P(("row", "col"), None, None, None),
        check_vma=False,
    )
```

```python
import functools

import jax
import jax.numpy as jnp
from jax import lax
from jax.experimental import pallas as pl
from jax.experimental.pallas import tpu as pltpu
from jax.sharding import PartitionSpec as P

W = 8
HALVES = 4
MESH = pl.DeviceIdType.MESH


def kernel(rows, cols, per, own_ref, order_ref, occ_ref, out_ref, stage, gat, raw, wgt, res, hop, in_sem, fsem, psem, rsem, gsem, xsem, ysem, usem, osem, qsem, hsem, ssem):
    row, z = lax.axis_index("row"), lax.axis_index("col")
    k = lax.rem(row, per)
    base = row - k
    place = k * cols + z
    size = per * cols
    halves = raw.shape[1]
    units = cols * halves
    mid = cols // 2
    has_up, has_down = row + per < rows, row >= per
    has_up2, has_down2 = row + 2 * per < rows, row >= 2 * per
    odd = lax.rem(row // per, 2) == 1
    ships_up = has_up & jnp.logical_not(odd) & ((place > 0) | has_down)
    ships_down = has_down & jnp.where(odd, (place < size - 1) | has_up, (place < size - 1) & jnp.logical_not(has_up))
    relays_up = has_up2 & (place > 0) & jnp.logical_not(odd)
    relays_down = has_down2 & (place < size - 1) & odd
    lower, upper = has_down & (place > 0), has_up & (place < size - 1)
    own_done = (jnp.minimum(z, cols - 1 - z) + 1) * halves - 1
    edge = (z == 0) | (z == cols - 1)
    direct = (odd, jnp.logical_not(odd) | jnp.logical_not(has_up2))
    bends = (jnp.logical_not(odd) & has_down2, odd & has_up2)
    carries = (jnp.logical_not(odd) & has_up2, odd & has_down2)
    bend_step = jnp.minimum(own_done + 2, units - 1)
    away_step = [jnp.minimum(jnp.where(d, own_done + 1, own_done + 2), units - 1) for d in direct]

    def remote(src, dst, send, recv, device):
        return pltpu.make_async_remote_copy(
            src_ref=src, dst_ref=dst, send_sem=send, recv_sem=recv, device_id=device, device_id_type=MESH
        )

    def onward(way, v, c):
        there = lax.rem(z + 1 - 2 * way + cols, cols)
        return remote(gat.at[k, v, c], gat.at[k, v, c], fsem.at[way, c], rsem.at[v, c], (row, there))

    def partner(d, v, c):
        there = base + lax.rem(k + d, per)
        return remote(gat.at[k, v, c], gat.at[k, v, c], psem.at[d - 1], gsem.at[k, v], (there, z))

    def ship(way, h, c):
        there = lax.rem(row + (1 - 2 * way) * per + rows, rows)
        return remote(gat.at[k, z * halves + h, c], raw.at[way, h, c], xsem.at[way], usem.at[way, h, c], (there, z))

    def relay(way, h, c):
        there = lax.rem(row + (2 - 4 * way) * per + 2 * rows, rows)
        return remote(raw.at[1 - way, h, c], raw.at[way, h, c], ysem, usem.at[way, h, c], (there, z))

    def taken(way, h, c):
        remote(raw.at[way, h, c], raw.at[way, h, c], xsem.at[0], usem.at[way, h, c], (row, z)).wait_recv()

    def arrive(v, c):
        remote(gat.at[k, v, c], gat.at[k, v, c], xsem.at[0], rsem.at[v, c], (row, z)).wait_recv()

    def arrive_whole(kk, v):
        remote(gat.at[kk, v], gat.at[kk, v], xsem.at[0], gsem.at[kk, v], (row, z)).wait_recv()

    def sent_whole(ref, sem):
        remote(ref, ref, sem, xsem.at[0], (row, z)).wait_send()

    def ship_on(h, c, act):
        @pl.when(ships_up)
        def _():
            act(ship(0, h, c))

        @pl.when(ships_down)
        def _():
            act(ship(1, h, c))

    def start(copy):
        copy.start()

    fill = pltpu.make_async_copy(own_ref, stage, in_sem)
    fill.start()
    barrier = pltpu.get_barrier_semaphore()
    for d in range(1, per):
        pl.semaphore_signal(barrier, inc=1, device_id=(base + lax.rem(k + d, per), z), device_id_type=MESH)

    greeted = per - 1
    for present, step in ((z < cols - 1, 1), (z > 0, -1)):
        greeted = greeted + present.astype(jnp.int32)

        @pl.when(present)
        def _():
            pl.semaphore_signal(barrier, inc=1, device_id=(row, lax.rem(z + step + cols, cols)), device_id_type=MESH)

    for present, step in ((has_up, per), (has_down, -per), (has_up2, 2 * per), (has_down2, -2 * per)):
        greeted = greeted + present.astype(jnp.int32)

        @pl.when(present)
        def _():
            there = lax.rem(row + step + 2 * rows, rows)
            pl.semaphore_signal(barrier, inc=1, device_id=(there, z), device_id_type=MESH)

    fill.wait()

    first = row * cols

    @pl.loop(0, cols)
    def _(i):
        pick = jnp.clip(order_ref[first + i] - first, 0, cols - 1)

        @pl.loop(0, halves)
        def _(h):
            rows_of = stage.shape[1] // halves
            gat[k, i * halves + h, z] = stage[pick, pl.ds(pl.multiple_of(h * rows_of, rows_of), rows_of)]

    pl.semaphore_wait(barrier, greeted)

    def early(n):
        return 2 * n < units - 1

    def due(way, v, n):
        if way == 0:
            return (z < cols - 1) & jnp.where(z + 1 >= mid, v == units - 1 - n, early(n))
        return (z > 0) & jnp.where(z - 1 < mid, v == n, early(n))

    def awaited(way, v, n):
        if way == 0:
            return jnp.where(z >= mid, v == units - 1 - n, early(n))
        return jnp.where(z < mid, v == n, early(n))

    def own_sends(way, m):
        for v in (units - 1 - m, m) if way == 0 else (m, units - 1 - m):

            @pl.when(due(way, v, m))
            def _():
                onward(way, v, z).start()

    ahead = (jnp.where(z == 0, units, z), jnp.where(z == cols - 1, units, cols - 1 - z))
    for way in (0, 1):

        @pl.loop(0, jnp.minimum(ahead[way], units))
        def _(m):
            own_sends(way, m)

    @pl.loop(0, halves)
    def _(h):
        ship_on(h, z, start)

    @pl.loop(0, units)
    def _(v):
        for d in range(1, per):
            partner(d, v, z).start()

    def got(v, c):
        arrive(v, c)
        for d in range(1, per):
            partner(d, v, c).start()

        @pl.when(v // halves == z)
        def _():
            ship_on(lax.rem(v, halves), c, start)

    def queue_own(n):
        for way in (0, 1):

            @pl.when(n + ahead[way] < units)
            def _():
                own_sends(way, n + ahead[way])

    def gather(n, far):
        @pl.loop(1, cols)
        def _(s):
            lanes = ((0, units - 1 - n, z < mid), (1, n, z >= mid), (0, n, None), (1, units - 1 - n, None))
            for way, v, is_far in lanes:
                if far and is_far is None:
                    continue
                c = z - s if way == 0 else z + s
                there = c >= 0 if way == 0 else c < cols
                if is_far is not None:
                    there = there & (is_far if far else jnp.logical_not(is_far))

                @pl.when(there & awaited(way, v, n))
                def _():
                    got(v, c)

                @pl.when(there & due(way, v, n))
                def _():
                    onward(way, v, c).start()

    def relay_on(h, c, act):
        @pl.when(relays_up)
        def _():
            act(relay(0, h, c), 1)

        @pl.when(relays_down)
        def _():
            act(relay(1, h, c), 0)

    def receive_and_relay(h, c):
        def act(copy, way):
            taken(way, h, c)
            copy.start()

        relay_on(h, c, act)

    def ship_step(h, c):
        v = z * halves + h
        middle = jnp.minimum(v, units - 1 - v)
        below = jnp.where(z >= mid, units - 1 - v, middle)
        above = jnp.where(z < mid, v, middle)
        return jnp.where(c == z, 0, jnp.where(c < z, below, above))

    def relay_due(n):
        def maybe(h, c):
            @pl.when((c >= 0) & (c < cols) & (ship_step(h, c) == n))
            def _():
                receive_and_relay(h, c)

        @pl.loop(0, halves)
        def _(h):
            maybe(h, z)

            @pl.loop(1, cols)
            def _(s):
                maybe(h, z - s)
                maybe(h, z + s)

    def scale(way, source):
        rows_of = wgt.shape[2] // halves
        for h in range(halves):

            @pl.loop(0, cols)
            def _(c):
                wgt[way, c, h * rows_of : (h + 1) * rows_of] = (source(h, c).astype(jnp.float32) * occ_ref[c]).astype(jnp.bfloat16)

    def prepare_away(way):
        present, waited = ((lower, relays_down), (upper, relays_up))[way]

        @pl.when(present)
        def _():
            @pl.when(jnp.logical_not(waited))
            def _():
                @pl.loop(0, halves)
                def _(h):
                    @pl.loop(0, cols)
                    def _(c):
                        taken(way, h, c)

            scale(way, lambda h, c: raw[way, h, c])

    def prepare_home():
        scale(2, lambda h, c: gat[k, z * halves + h, c])

    def answer(t):
        low = t < place
        other = jnp.where(low, t, t + 1)
        slot = jnp.where(low, size + other - place, other - place - size) + W - 1
        near = (slot >= 0) & (slot < 2 * W - 1)
        return low, other, slot, near

    def reply(t, h):
        low, other, slot, near = answer(t)
        there = lax.rem(jnp.where(low, row - per, row + per) + rows, rows)
        go = near & jnp.where(low, row - per >= 0, row + per < rows)
        slot = jnp.clip(slot, 0, 2 * W - 2)
        return go, remote(res.at[t, h], out_ref.at[slot, h], osem.at[t], qsem.at[slot], (there, z))

    def bend(way, t, h):
        there = lax.rem(row + (4 * way - 2) * per + 2 * rows, rows)
        return remote(res.at[t, h], hop.at[t, h], osem.at[t], hsem.at[t, h], (there, z))

    def carry(way, t, h):
        low, other, slot, near = answer(t)
        there = lax.rem(row + (1 - 2 * way) * per + rows, rows)
        slot = jnp.clip(slot, 0, 2 * W - 2)
        go = carries[way] & near & (low if way == 0 else jnp.logical_not(low))
        return go, remote(hop.at[t, h], out_ref.at[slot, h], ssem.at[t], qsem.at[slot], (there, z))

    def bent(m):
        return lax.rem(m, 2) == 0

    def unit(n):
        return jnp.where(z < mid, n, units - 1 - n)

    def local(t, h):
        other = t - (size - 1)
        slot = other - place + W - 1
        near = (slot >= 0) & (slot < 2 * W - 1)
        slot = jnp.clip(slot, 0, 2 * W - 2)
        return near, pltpu.make_async_copy(res.at[t, h], out_ref.at[slot, h], osem.at[t])

    def product(t, way, kk, v):
        total = jnp.zeros(res.shape[2:], jnp.float32)
        for c in range(cols):
            total = total + lax.dot_general(
                wgt[way, c], gat[kk, v, c], (((1,), (1,)), ((), ())), preferred_element_type=jnp.float32
            )
        res[t, lax.rem(v, halves)] = total.astype(jnp.bfloat16)

    def home(kk, m):
        v = unit(m)
        t = kk * cols + v // halves + size - 1
        near, copy = local(t, lax.rem(v, halves))

        @pl.when(near)
        def _():
            product(t, 2, kk, v)
            copy.start()

    def away(way, kk, m):
        v = unit(m)
        other = kk * cols + v // halves
        t = jnp.clip(other - way, 0, size - 2)
        go, copy = reply(t, lax.rem(v, halves))

        @pl.when(go & ((other < place) if way == 0 else (other > place)))
        def _():
            product(t, way, kk, v)
            bends_now = bends[way] & bent(m)

            @pl.when(bends_now)
            def _():
                bend(way, t, lax.rem(v, halves)).start()

            @pl.when(jnp.logical_not(bends_now))
            def _():
                copy.start()

    def carry_due(n):
        def one(m):
            v = unit(m)
            h = lax.rem(v, halves)
            for way in (0, 1):

                @pl.loop(0, per)
                def _(kk):
                    other = kk * cols + v // halves
                    t = jnp.clip(other - way, 0, size - 2)
                    go, copy = carry(way, t, h)

                    @pl.when(go & ((other < place) if way == 0 else (other > place)) & bent(m))
                    def _():
                        remote(hop.at[t, h], hop.at[t, h], xsem.at[0], hsem.at[t, h], (row, z)).wait_recv()
                        copy.start()

        @pl.when(n > bend_step)
        def _():
            @pl.loop(jnp.where(n == bend_step + 1, 0, n - 1), n)
            def _(m):
                one(m)

    def work(n, since, prepare, each):
        @pl.when(n == since)
        def _():
            prepare()

        @pl.when(n >= since)
        def _():
            @pl.loop(jnp.where(n == since, 0, n), n + 1)
            def _(m):
                @pl.loop(0, per)
                def _(kk):
                    each(kk, m)

    gather(0, True)

    @pl.loop(0, units)
    def _(n):
        @pl.when(edge)
        def _():
            carry_due(n)

        queue_own(n)
        gather(n, False)

        @pl.when(n + 1 < units)
        def _():
            gather(n + 1, True)

        @pl.when(jnp.logical_not(edge))
        def _():
            carry_due(n)

        for d in range(1, per):
            arrive_whole(lax.rem(k + d, per), unit(n))

        for way in (0, 1):
            work(n, away_step[way], functools.partial(prepare_away, way), functools.partial(away, way))
        work(n, own_done, prepare_home, home)
        relay_due(n)

    carry_due(units)

    @pl.loop(0, cols)
    def _(c):
        @pl.when((z < cols - 1) & (c <= z))
        def _():
            sent_whole(gat.at[k, :, c], fsem.at[0, c])

        @pl.when((z > 0) & (c >= z))
        def _():
            sent_whole(gat.at[k, :, c], fsem.at[1, c])

    for d in range(1, per):
        sent_whole(gat.at[k], psem.at[d - 1])

    for way, shipped, relayed in ((0, ships_up, relays_up), (1, ships_down, relays_down)):

        @pl.when(shipped)
        def _():
            sent_whole(raw.at[way], xsem.at[way])

        @pl.when(relayed)
        def _():
            sent_whole(raw.at[way], ysem)

    @pl.loop(0, size - 1)
    def _(t):
        low, other, slot, near = answer(t)
        slot = jnp.clip(slot, 0, 2 * W - 2)

        @pl.when(near & jnp.where(low, has_down, has_up))
        def _():
            sent_whole(res.at[t], osem.at[t])

        @pl.when(near & jnp.where(low, carries[0], carries[1]))
        def _():
            sent_whole(hop.at[t, : halves // 2], ssem.at[t])

        @pl.when(near & jnp.where(low, has_up, has_down))
        def _():
            remote(out_ref.at[slot], out_ref.at[slot], xsem.at[0], qsem.at[slot], (row, z)).wait_recv()

    @pl.loop(size - 1, 2 * size - 1)
    def _(t):
        slot = t - (size - 1) - place + W - 1

        @pl.when((slot >= 0) & (slot < 2 * W - 1))
        def _():
            pltpu.make_async_copy(res.at[t], out_ref.at[jnp.clip(slot, 0, 2 * W - 2)], osem.at[t]).wait()


def place_blocks(neighbours_ref, counts_ref, block_ref, out_ref, held, blank, in_sem, out_sem):
    here = lax.axis_index("row") * lax.axis_size("col") + lax.axis_index("col")
    halves, wide = block_ref.shape[1], block_ref.shape[3]
    blank[...] = jnp.zeros_like(blank)

    def fetch(j, h):
        at = jnp.clip(neighbours_ref[0, j] - here + (W - 1), 0, 2 * W - 2)
        return pltpu.make_async_copy(block_ref.at[at, h], held.at[j, :, pl.ds(h * wide, wide)], in_sem.at[j, h])

    def store(j, source):
        return pltpu.make_async_copy(source, out_ref.at[j], out_sem.at[j])

    slots = out_ref.shape[0]
    for j in range(slots):

        @pl.when(j < counts_ref[0])
        def _():
            for h in range(halves):
                fetch(j, h).start()

        @pl.when(j >= counts_ref[0])
        def _():
            store(j, blank).start()

    for j in range(slots):

        @pl.when(j < counts_ref[0])
        def _():
            for h in range(halves):
                fetch(j, h).wait()
            store(j, held.at[j]).start()

    for j in range(slots):
        store(j, blank).wait()


def shards(coeffs, occupations, block_order, neighbours, counts):
    rows, cols = lax.axis_size("row"), lax.axis_size("col")
    states = coeffs.shape[1]
    depth = coeffs.shape[0] // cols
    per = -(-W // cols)
    size = per * cols
    units, half = cols * HALVES, depth // HALVES
    slots_total = 2 * W - 1
    own = coeffs.reshape(cols, depth, states)
    occ = occupations.reshape(cols, 1, states)
    dma = pltpu.SemaphoreType.DMA
    blocks = pl.pallas_call(
        functools.partial(kernel, rows, cols, per),
        out_shape=jax.ShapeDtypeStruct((slots_total, HALVES, depth, half), jnp.bfloat16),
        in_specs=[
            pl.BlockSpec(memory_space=pl.ANY),
            pl.BlockSpec(memory_space=pltpu.SMEM),
            pl.BlockSpec(memory_space=pltpu.VMEM),
        ],
        out_specs=pl.BlockSpec(memory_space=pl.ANY),
        scratch_shapes=[
            pltpu.VMEM((cols, depth, states), jnp.bfloat16),
            pltpu.VMEM((per, units, cols, half, states), jnp.bfloat16),
            pltpu.VMEM((2, HALVES, cols, half, states), jnp.bfloat16),
            pltpu.VMEM((3, cols, depth, states), jnp.bfloat16),
            pltpu.VMEM((2 * size - 1, HALVES, depth, half), jnp.bfloat16),
            pltpu.VMEM((size - 1, HALVES, depth, half), jnp.bfloat16),
            dma,
            dma((2, cols)),
            dma((max(per - 1, 1),)),
            dma((units, cols)),
            dma((per, units)),
            dma((2,)),
            dma,
            dma((2, HALVES, cols)),
            dma((2 * size - 1,)),
            dma((slots_total,)),
            dma((size - 1, HALVES)),
            dma((size - 1,)),
        ],
        compiler_params=pltpu.CompilerParams(
            collective_id=0, has_side_effects=True, vmem_limit_bytes=60 * 1024 * 1024
        ),
        name="density_blocks",
    )(own, block_order, occ)
    slots = neighbours.shape[1]
    placed = pl.pallas_call(
        place_blocks,
        out_shape=jax.ShapeDtypeStruct((slots, depth, depth), jnp.bfloat16),
        in_specs=[
            pl.BlockSpec(memory_space=pltpu.SMEM),
            pl.BlockSpec(memory_space=pltpu.SMEM),
            pl.BlockSpec(memory_space=pl.ANY),
        ],
        out_specs=pl.BlockSpec(memory_space=pl.ANY),
        scratch_shapes=[
            pltpu.VMEM((slots, depth, depth), jnp.bfloat16),
            pltpu.VMEM((depth, depth), jnp.bfloat16),
            dma((slots, HALVES)),
            dma((slots,)),
        ],
        name="place_blocks",
    )(neighbours, counts, blocks)
    return placed[None]


def solution(mesh):
    return jax.shard_map(
        shards,
        mesh=mesh,
        in_specs=(P("row", "col"), P(), P(), P(("row", "col"), None), P(("row", "col"))),
        out_specs=P(("row", "col"), None, None, None),
        check_vma=False,
    )
```

```python
import functools

import jax
import jax.numpy as jnp
from jax import lax
from jax.experimental import pallas as pl
from jax.experimental.pallas import tpu as pltpu
from jax.sharding import PartitionSpec as P

W = 8
HALVES = 4
VMEM_MIB = 44
MESH = pl.DeviceIdType.MESH


def kernel(rows, cols, per, own_ref, order_in, occ_in, out_ref, order_ref, occ_ref, stage, gat, raw, wgt, res, hop, order_sem, occ_sem, in_sem, fsem, psem, rsem, gsem, xsem, ysem, usem, osem, qsem, hsem, ssem):
    row, z = lax.axis_index("row"), lax.axis_index("col")
    k = lax.rem(row, per)
    base = row - k
    place = k * cols + z
    size = per * cols
    halves = raw.shape[1]
    units = cols * halves
    mid = cols // 2
    has_up, has_down = row + per < rows, row >= per
    has_up2, has_down2 = row + 2 * per < rows, row >= 2 * per
    odd = lax.rem(row // per, 2) == 1
    ships_up = has_up & jnp.logical_not(odd) & ((place > 0) | has_down)
    ships_down = has_down & jnp.where(odd, (place < size - 1) | has_up, (place < size - 1) & jnp.logical_not(has_up))
    relays_up = has_up2 & (place > 0) & jnp.logical_not(odd)
    relays_down = has_down2 & (place < size - 1) & odd
    lower, upper = has_down & (place > 0), has_up & (place < size - 1)
    own_done = (jnp.minimum(z, cols - 1 - z) + 1) * halves - 1
    edge = (z == 0) | (z == cols - 1)
    direct = (odd, jnp.logical_not(odd) | jnp.logical_not(has_up2))
    bends = (jnp.logical_not(odd) & has_down2, odd & has_up2)
    carries = (jnp.logical_not(odd) & has_up2, odd & has_down2)
    bend_step = jnp.minimum(own_done + 2, units - 1)
    away_step = [jnp.minimum(jnp.where(d, own_done + 1, own_done + 2), units - 1) for d in direct]

    def remote(src, dst, send, recv, device):
        return pltpu.make_async_remote_copy(
            src_ref=src, dst_ref=dst, send_sem=send, recv_sem=recv, device_id=device, device_id_type=MESH
        )

    def onward(way, v, c):
        there = lax.rem(z + 1 - 2 * way + cols, cols)
        return remote(gat.at[k, v, c], gat.at[k, v, c], fsem.at[way, c], rsem.at[v, c], (row, there))

    def partner(d, v, c):
        there = base + lax.rem(k + d, per)
        return remote(gat.at[k, v, c], gat.at[k, v, c], psem.at[d - 1], gsem.at[k, v], (there, z))

    def ship(way, h, c):
        there = lax.rem(row + (1 - 2 * way) * per + rows, rows)
        return remote(gat.at[k, z * halves + h, c], raw.at[way, h, c], xsem.at[way], usem.at[way, h, c], (there, z))

    def relay(way, h, c):
        there = lax.rem(row + (2 - 4 * way) * per + 2 * rows, rows)
        return remote(raw.at[1 - way, h, c], raw.at[way, h, c], ysem, usem.at[way, h, c], (there, z))

    def taken(way, h, c):
        remote(raw.at[way, h, c], raw.at[way, h, c], xsem.at[0], usem.at[way, h, c], (row, z)).wait_recv()

    def arrive(v, c):
        remote(gat.at[k, v, c], gat.at[k, v, c], xsem.at[0], rsem.at[v, c], (row, z)).wait_recv()

    def arrive_whole(kk, v):
        remote(gat.at[kk, v], gat.at[kk, v], xsem.at[0], gsem.at[kk, v], (row, z)).wait_recv()

    def sent_whole(ref, sem):
        remote(ref, ref, sem, xsem.at[0], (row, z)).wait_send()

    def ship_on(h, c, act):
        @pl.when(ships_up)
        def _():
            act(ship(0, h, c))

        @pl.when(ships_down)
        def _():
            act(ship(1, h, c))

    def start(copy):
        copy.start()

    order_copy = pltpu.make_async_copy(order_in, order_ref, order_sem)
    occ_copy = pltpu.make_async_copy(occ_in, occ_ref, occ_sem)
    fills = []
    for i in range(cols):
        for h in range(halves):
            part = pl.ds(h * (stage.shape[1] // halves), stage.shape[1] // halves)
            fills.append(pltpu.make_async_copy(own_ref.at[i, part], stage.at[i, part], in_sem.at[i * halves + h]))
    order_copy.start()
    for fill in fills:
        fill.start()
    occ_copy.start()
    barrier = pltpu.get_barrier_semaphore()
    for d in range(1, per):
        pl.semaphore_signal(barrier, inc=1, device_id=(base + lax.rem(k + d, per), z), device_id_type=MESH)

    greeted = per - 1
    for present, step in ((z < cols - 1, 1), (z > 0, -1)):
        greeted = greeted + present.astype(jnp.int32)

        @pl.when(present)
        def _():
            pl.semaphore_signal(barrier, inc=1, device_id=(row, lax.rem(z + step + cols, cols)), device_id_type=MESH)

    for present, step in ((has_up, per), (has_down, -per), (has_up2, 2 * per), (has_down2, -2 * per)):
        greeted = greeted + present.astype(jnp.int32)

        @pl.when(present)
        def _():
            there = lax.rem(row + step + 2 * rows, rows)
            pl.semaphore_signal(barrier, inc=1, device_id=(there, z), device_id_type=MESH)

    order_copy.wait()
    for fill in fills:
        fill.wait()
    occ_copy.wait()

    first = row * cols

    @pl.loop(0, cols)
    def _(i):
        pick = jnp.clip(order_ref[first + i] - first, 0, cols - 1)

        @pl.loop(0, halves)
        def _(h):
            rows_of = stage.shape[1] // halves
            gat[k, i * halves + h, z] = stage[pick, pl.ds(pl.multiple_of(h * rows_of, rows_of), rows_of)]

    pl.semaphore_wait(barrier, greeted)

    def early(n):
        return 2 * n < units - 1

    def due(way, v, n):
        if way == 0:
            return (z < cols - 1) & jnp.where(z + 1 >= mid, v == units - 1 - n, early(n))
        return (z > 0) & jnp.where(z - 1 < mid, v == n, early(n))

    def awaited(way, v, n):
        if way == 0:
            return jnp.where(z >= mid, v == units - 1 - n, early(n))
        return jnp.where(z < mid, v == n, early(n))

    def own_sends(way, m):
        for v in (units - 1 - m, m) if way == 0 else (m, units - 1 - m):

            @pl.when(due(way, v, m))
            def _():
                onward(way, v, z).start()

    ahead = (jnp.where(z == 0, units, z), jnp.where(z == cols - 1, units, cols - 1 - z))
    for way in (0, 1):

        @pl.loop(0, jnp.minimum(ahead[way], units))
        def _(m):
            own_sends(way, m)

    @pl.loop(0, halves)
    def _(h):
        ship_on(h, z, start)

    @pl.loop(0, units)
    def _(v):
        for d in range(1, per):
            partner(d, v, z).start()

    def got(v, c):
        arrive(v, c)
        for d in range(1, per):
            partner(d, v, c).start()

        @pl.when(v // halves == z)
        def _():
            ship_on(lax.rem(v, halves), c, start)

    def queue_own(n):
        for way in (0, 1):

            @pl.when(n + ahead[way] < units)
            def _():
                own_sends(way, n + ahead[way])

    def gather(n, far):
        @pl.loop(1, cols)
        def _(s):
            lanes = ((0, units - 1 - n, z < mid), (1, n, z >= mid), (0, n, None), (1, units - 1 - n, None))
            for way, v, is_far in lanes:
                if far and is_far is None:
                    continue
                c = z - s if way == 0 else z + s
                there = c >= 0 if way == 0 else c < cols
                if is_far is not None:
                    there = there & (is_far if far else jnp.logical_not(is_far))

                @pl.when(there & awaited(way, v, n))
                def _():
                    got(v, c)

                @pl.when(there & due(way, v, n))
                def _():
                    onward(way, v, c).start()

    def relay_on(h, c, act):
        @pl.when(relays_up)
        def _():
            act(relay(0, h, c), 1)

        @pl.when(relays_down)
        def _():
            act(relay(1, h, c), 0)

    def receive_and_relay(h, c):
        def act(copy, way):
            taken(way, h, c)
            copy.start()

        relay_on(h, c, act)

    def ship_step(h, c):
        v = z * halves + h
        middle = jnp.minimum(v, units - 1 - v)
        below = jnp.where(z >= mid, units - 1 - v, middle)
        above = jnp.where(z < mid, v, middle)
        return jnp.where(c == z, 0, jnp.where(c < z, below, above))

    def relay_due(n):
        def maybe(h, c):
            @pl.when((c >= 0) & (c < cols) & (ship_step(h, c) == n))
            def _():
                receive_and_relay(h, c)

        @pl.loop(0, halves)
        def _(h):
            maybe(h, z)

            @pl.loop(1, cols)
            def _(s):
                maybe(h, z - s)
                maybe(h, z + s)

    def scale(way, source):
        rows_of = wgt.shape[2] // halves
        for h in range(halves):

            @pl.loop(0, cols)
            def _(c):
                wgt[way, c, h * rows_of : (h + 1) * rows_of] = (source(h, c).astype(jnp.float32) * occ_ref[c]).astype(jnp.bfloat16)

    def prepare_away(way):
        present, waited = ((lower, relays_down), (upper, relays_up))[way]

        @pl.when(present)
        def _():
            @pl.when(jnp.logical_not(waited))
            def _():
                @pl.loop(0, halves)
                def _(h):
                    @pl.loop(0, cols)
                    def _(c):
                        taken(way, h, c)

            scale(way, lambda h, c: raw[way, h, c])

    def prepare_home():
        scale(2, lambda h, c: gat[k, z * halves + h, c])

    def answer(t):
        low = t < place
        other = jnp.where(low, t, t + 1)
        slot = jnp.where(low, size + other - place, other - place - size) + W - 1
        near = (slot >= 0) & (slot < 2 * W - 1)
        return low, other, slot, near

    def reply(t, h):
        low, other, slot, near = answer(t)
        there = lax.rem(jnp.where(low, row - per, row + per) + rows, rows)
        go = near & jnp.where(low, row - per >= 0, row + per < rows)
        slot = jnp.clip(slot, 0, 2 * W - 2)
        return go, remote(res.at[t, h], out_ref.at[slot, h], osem.at[t], qsem.at[slot], (there, z))

    def bend(way, t, h):
        there = lax.rem(row + (4 * way - 2) * per + 2 * rows, rows)
        return remote(res.at[t, h], hop.at[t, h], osem.at[t], hsem.at[t, h], (there, z))

    def carry(way, t, h):
        low, other, slot, near = answer(t)
        there = lax.rem(row + (1 - 2 * way) * per + rows, rows)
        slot = jnp.clip(slot, 0, 2 * W - 2)
        go = carries[way] & near & (low if way == 0 else jnp.logical_not(low))
        return go, remote(hop.at[t, h], out_ref.at[slot, h], ssem.at[t], qsem.at[slot], (there, z))

    def bent(m):
        return lax.rem(m, 2) == 0

    def unit(n):
        return jnp.where(z < mid, n, units - 1 - n)

    def product(way, kk, v, target):
        total = jnp.zeros(target.shape, jnp.float32)
        for c in range(cols):
            total = total + lax.dot_general(
                wgt[way, c], gat[kk, v, c], (((1,), (1,)), ((), ())), preferred_element_type=jnp.float32
            )
        target[...] = total.astype(jnp.bfloat16)

    def home(kk, m):
        v = unit(m)
        slot = kk * cols + v // halves - place + W - 1

        @pl.when((slot >= 0) & (slot < 2 * W - 1))
        def _():
            product(2, kk, v, out_ref.at[jnp.clip(slot, 0, 2 * W - 2), lax.rem(v, halves)])

    def away(way, kk, m):
        v = unit(m)
        other = kk * cols + v // halves
        t = jnp.clip(other - way, 0, size - 2)
        go, copy = reply(t, lax.rem(v, halves))

        @pl.when(go & ((other < place) if way == 0 else (other > place)))
        def _():
            product(way, kk, v, res.at[t, lax.rem(v, halves)])
            bends_now = bends[way] & bent(m)

            @pl.when(bends_now)
            def _():
                bend(way, t, lax.rem(v, halves)).start()

            @pl.when(jnp.logical_not(bends_now))
            def _():
                copy.start()

    def carry_due(n):
        def one(m):
            v = unit(m)
            h = lax.rem(v, halves)
            for way in (0, 1):

                @pl.loop(0, per)
                def _(kk):
                    other = kk * cols + v // halves
                    t = jnp.clip(other - way, 0, size - 2)
                    go, copy = carry(way, t, h)

                    @pl.when(go & ((other < place) if way == 0 else (other > place)) & bent(m))
                    def _():
                        remote(hop.at[t, h], hop.at[t, h], xsem.at[0], hsem.at[t, h], (row, z)).wait_recv()
                        copy.start()

        @pl.when(n > bend_step)
        def _():
            @pl.loop(jnp.where(n == bend_step + 1, 0, n - 1), n)
            def _(m):
                one(m)

    def work(n, since, prepare, each):
        @pl.when(n == since)
        def _():
            prepare()

        @pl.when(n >= since)
        def _():
            @pl.loop(jnp.where(n == since, 0, n), n + 1)
            def _(m):
                @pl.loop(0, per)
                def _(kk):
                    each(kk, m)

    gather(0, True)

    @pl.loop(0, units)
    def _(n):
        @pl.when(edge)
        def _():
            carry_due(n)

        queue_own(n)
        gather(n, False)

        @pl.when(n + 1 < units)
        def _():
            gather(n + 1, True)

        @pl.when(jnp.logical_not(edge))
        def _():
            carry_due(n)

        for d in range(1, per):
            arrive_whole(lax.rem(k + d, per), unit(n))

        for way in (0, 1):
            work(n, away_step[way], functools.partial(prepare_away, way), functools.partial(away, way))
        work(n, own_done, prepare_home, home)
        relay_due(n)

    carry_due(units)

    @pl.loop(0, cols)
    def _(c):
        @pl.when((z < cols - 1) & (c <= z))
        def _():
            sent_whole(gat.at[k, :, c], fsem.at[0, c])

        @pl.when((z > 0) & (c >= z))
        def _():
            sent_whole(gat.at[k, :, c], fsem.at[1, c])

    for d in range(1, per):
        sent_whole(gat.at[k], psem.at[d - 1])

    for way, shipped, relayed in ((0, ships_up, relays_up), (1, ships_down, relays_down)):

        @pl.when(shipped)
        def _():
            sent_whole(raw.at[way], xsem.at[way])

        @pl.when(relayed)
        def _():
            sent_whole(raw.at[way], ysem)

    @pl.loop(0, size - 1)
    def _(t):
        low, other, slot, near = answer(t)
        slot = jnp.clip(slot, 0, 2 * W - 2)

        @pl.when(near & jnp.where(low, has_down, has_up))
        def _():
            sent_whole(res.at[t], osem.at[t])

        @pl.when(near & jnp.where(low, carries[0], carries[1]))
        def _():
            sent_whole(hop.at[t, : halves // 2], ssem.at[t])

        @pl.when(near & jnp.where(low, has_up, has_down))
        def _():
            remote(out_ref.at[slot], out_ref.at[slot], xsem.at[0], qsem.at[slot], (row, z)).wait_recv()


def place_blocks(neighbours_ref, counts_ref, block_ref, out_ref, blank, out_sem):
    here = lax.axis_index("row") * lax.axis_size("col") + lax.axis_index("col")
    halves, wide = block_ref.shape[1], block_ref.shape[3]
    blank[...] = jnp.zeros_like(blank)

    def store(j, h):
        at = jnp.clip(neighbours_ref[0, j] - here + (W - 1), 0, 2 * W - 2)
        return pltpu.make_async_copy(block_ref.at[at, h], out_ref.at[j, :, pl.ds(h * wide, wide)], out_sem.at[j])

    slots = out_ref.shape[0]
    for j in range(slots):

        @pl.when(j < counts_ref[0])
        def _():
            for h in range(halves):
                store(j, h).start()

        @pl.when(j >= counts_ref[0])
        def _():
            pltpu.make_async_copy(blank, out_ref.at[j], out_sem.at[j]).start()

    for j in range(slots):
        pltpu.make_async_copy(blank, out_ref.at[j], out_sem.at[j]).wait()


def shards(coeffs, occupations, block_order, neighbours, counts):
    rows, cols = lax.axis_size("row"), lax.axis_size("col")
    states = coeffs.shape[1]
    depth = coeffs.shape[0] // cols
    per = -(-W // cols)
    size = per * cols
    units, half = cols * HALVES, depth // HALVES
    slots_total = 2 * W - 1
    own = coeffs.reshape(cols, depth, states)
    occ = occupations.reshape(cols, 1, states)
    dma = pltpu.SemaphoreType.DMA
    blocks = pl.pallas_call(
        functools.partial(kernel, rows, cols, per),
        out_shape=jax.ShapeDtypeStruct((slots_total, HALVES, depth, half), jnp.bfloat16),
        in_specs=[
            pl.BlockSpec(memory_space=pltpu.HBM),
            pl.BlockSpec(memory_space=pltpu.HBM),
            pl.BlockSpec(memory_space=pltpu.HBM),
        ],
        out_specs=pl.BlockSpec(memory_space=pltpu.VMEM),
        scratch_shapes=[
            pltpu.SMEM(block_order.shape, block_order.dtype),
            pltpu.VMEM(occ.shape, occ.dtype),
            pltpu.VMEM((cols, depth, states), jnp.bfloat16),
            pltpu.VMEM((per, units, cols, half, states), jnp.bfloat16),
            pltpu.VMEM((2, HALVES, cols, half, states), jnp.bfloat16),
            pltpu.VMEM((3, cols, depth, states), jnp.bfloat16),
            pltpu.VMEM((size - 1, HALVES, depth, half), jnp.bfloat16),
            pltpu.VMEM((size - 1, HALVES, depth, half), jnp.bfloat16),
            dma,
            dma,
            dma((units,)),
            dma((2, cols)),
            dma((max(per - 1, 1),)),
            dma((units, cols)),
            dma((per, units)),
            dma((2,)),
            dma,
            dma((2, HALVES, cols)),
            dma((size - 1,)),
            dma((slots_total,)),
            dma((size - 1, HALVES)),
            dma((size - 1,)),
        ],
        compiler_params=pltpu.CompilerParams(
            collective_id=0, has_side_effects=True, vmem_limit_bytes=VMEM_MIB * 1024 * 1024
        ),
        name="density_blocks",
    )(*(pltpu.with_memory_space_constraint(x, pltpu.HBM) for x in (own, block_order, occ)))
    slots = neighbours.shape[1]
    placed = pl.pallas_call(
        place_blocks,
        out_shape=jax.ShapeDtypeStruct((slots, depth, depth), jnp.bfloat16),
        in_specs=[
            pl.BlockSpec(memory_space=pltpu.SMEM),
            pl.BlockSpec(memory_space=pltpu.SMEM),
            pl.BlockSpec(memory_space=pltpu.VMEM),
        ],
        out_specs=pl.BlockSpec(memory_space=pl.ANY),
        scratch_shapes=[
            pltpu.VMEM((depth, depth), jnp.bfloat16),
            dma((slots,)),
        ],
        compiler_params=pltpu.CompilerParams(vmem_limit_bytes=16 * 1024 * 1024),
        name="place_blocks",
    )(neighbours, counts, blocks)
    return placed[None]


def solution(mesh):
    return jax.shard_map(
        shards,
        mesh=mesh,
        in_specs=(P("row", "col"), P(), P(), P(("row", "col"), None), P(("row", "col"))),
        out_specs=P(("row", "col"), None, None, None),
        check_vma=False,
    )
```

```python
import functools

import jax
import jax.numpy as jnp
from jax import lax
from jax.experimental import pallas as pl
from jax.experimental.pallas import tpu as pltpu
from jax.sharding import PartitionSpec as P

W = 8
HALVES = 4
VMEM_MIB = 44
MESH = pl.DeviceIdType.MESH


def kernel(rows, cols, per, own_ref, order_in, occ_in, out_ref, order_ref, occ_ref, stage, gat, raw, wgt, res, hop, order_sem, occ_sem, in_sem, fsem, psem, rsem, gsem, xsem, ysem, usem, osem, qsem, hsem, ssem):
    row, z = lax.axis_index("row"), lax.axis_index("col")
    k = lax.rem(row, per)
    base = row - k
    place = k * cols + z
    size = per * cols
    halves = raw.shape[1]
    units = cols * halves
    mid = cols // 2
    has_up, has_down = row + per < rows, row >= per
    has_up2, has_down2 = row + 2 * per < rows, row >= 2 * per
    odd = lax.rem(row // per, 2) == 1
    ships_up = has_up & jnp.logical_not(odd) & ((place > 0) | has_down)
    ships_down = has_down & jnp.where(odd, (place < size - 1) | has_up, (place < size - 1) & jnp.logical_not(has_up))
    relays_up = has_up2 & (place > 0) & jnp.logical_not(odd)
    relays_down = has_down2 & (place < size - 1) & odd
    lower, upper = has_down & (place > 0), has_up & (place < size - 1)
    own_done = (jnp.minimum(z, cols - 1 - z) + 1) * halves - 1
    edge = (z == 0) | (z == cols - 1)
    direct = (odd, jnp.logical_not(odd) | jnp.logical_not(has_up2))
    bends = (jnp.logical_not(odd) & has_down2, odd & has_up2)
    carries = (jnp.logical_not(odd) & has_up2, odd & has_down2)
    bend_step = jnp.minimum(own_done + 2, units - 1)
    away_step = [jnp.minimum(jnp.where(d, own_done + 1, own_done + 2), units - 1) for d in direct]

    def remote(src, dst, send, recv, device):
        return pltpu.make_async_remote_copy(
            src_ref=src, dst_ref=dst, send_sem=send, recv_sem=recv, device_id=device, device_id_type=MESH
        )

    def onward(way, v, c):
        there = lax.rem(z + 1 - 2 * way + cols, cols)
        return remote(gat.at[k, v, c], gat.at[k, v, c], fsem.at[way, c], rsem.at[v, c], (row, there))

    def partner(d, v, c):
        there = base + lax.rem(k + d, per)
        return remote(gat.at[k, v, c], gat.at[k, v, c], psem.at[d - 1], gsem.at[k, v], (there, z))

    def ship(way, h, c):
        there = lax.rem(row + (1 - 2 * way) * per + rows, rows)
        return remote(gat.at[k, z * halves + h, c], raw.at[way, h, c], xsem.at[way], usem.at[way, h, c], (there, z))

    def relay(way, h, c):
        there = lax.rem(row + (2 - 4 * way) * per + 2 * rows, rows)
        return remote(raw.at[1 - way, h, c], raw.at[way, h, c], ysem, usem.at[way, h, c], (there, z))

    def taken(way, h, c):
        remote(raw.at[way, h, c], raw.at[way, h, c], xsem.at[0], usem.at[way, h, c], (row, z)).wait_recv()

    def arrive(v, c):
        remote(gat.at[k, v, c], gat.at[k, v, c], xsem.at[0], rsem.at[v, c], (row, z)).wait_recv()

    def arrive_whole(kk, v):
        remote(gat.at[kk, v], gat.at[kk, v], xsem.at[0], gsem.at[kk, v], (row, z)).wait_recv()

    def sent_whole(ref, sem):
        remote(ref, ref, sem, xsem.at[0], (row, z)).wait_send()

    def ship_on(h, c, act):
        @pl.when(ships_up)
        def _():
            act(ship(0, h, c))

        @pl.when(ships_down)
        def _():
            act(ship(1, h, c))

    def start(copy):
        copy.start()

    order_copy = pltpu.make_async_copy(order_in, order_ref, order_sem)
    occ_copy = pltpu.make_async_copy(occ_in, occ_ref, occ_sem)
    fills = []
    for i in range(cols):
        for h in range(halves):
            part = pl.ds(h * (stage.shape[1] // halves), stage.shape[1] // halves)
            fills.append(pltpu.make_async_copy(own_ref.at[i, part], stage.at[i, part], in_sem.at[i * halves + h]))
    order_copy.start()
    for fill in fills:
        fill.start()
    occ_copy.start()
    barrier = pltpu.get_barrier_semaphore()
    for d in range(1, per):
        pl.semaphore_signal(barrier, inc=1, device_id=(base + lax.rem(k + d, per), z), device_id_type=MESH)

    greeted = per - 1
    for present, step in ((z < cols - 1, 1), (z > 0, -1)):
        greeted = greeted + present.astype(jnp.int32)

        @pl.when(present)
        def _():
            pl.semaphore_signal(barrier, inc=1, device_id=(row, lax.rem(z + step + cols, cols)), device_id_type=MESH)

    for present, step in ((has_up, per), (has_down, -per), (has_up2, 2 * per), (has_down2, -2 * per)):
        greeted = greeted + present.astype(jnp.int32)

        @pl.when(present)
        def _():
            there = lax.rem(row + step + 2 * rows, rows)
            pl.semaphore_signal(barrier, inc=1, device_id=(there, z), device_id_type=MESH)

    order_copy.wait()
    for fill in fills:
        fill.wait()
    occ_copy.wait()

    first = row * cols

    @pl.loop(0, cols)
    def _(i):
        pick = jnp.clip(order_ref[first + i] - first, 0, cols - 1)

        @pl.loop(0, halves)
        def _(h):
            rows_of = stage.shape[1] // halves
            gat[k, i * halves + h, z] = stage[pick, pl.ds(pl.multiple_of(h * rows_of, rows_of), rows_of)]

    pl.semaphore_wait(barrier, greeted)

    def early(n):
        return 2 * n < units - 1

    def due(way, v, n):
        if way == 0:
            return (z < cols - 1) & jnp.where(z + 1 >= mid, v == units - 1 - n, early(n))
        return (z > 0) & jnp.where(z - 1 < mid, v == n, early(n))

    def awaited(way, v, n):
        if way == 0:
            return jnp.where(z >= mid, v == units - 1 - n, early(n))
        return jnp.where(z < mid, v == n, early(n))

    def own_sends(way, m):
        for v in (units - 1 - m, m) if way == 0 else (m, units - 1 - m):

            @pl.when(due(way, v, m))
            def _():
                onward(way, v, z).start()

    ahead = (jnp.where(z == 0, units, z + 2 * (z >= mid)), jnp.where(z == cols - 1, units, cols - 1 - z + 2 * (z < mid)))
    for way in (0, 1):

        @pl.loop(0, jnp.minimum(ahead[way], units))
        def _(m):
            own_sends(way, m)

    @pl.loop(0, halves)
    def _(h):
        ship_on(h, z, start)

    @pl.loop(0, units)
    def _(v):
        for d in range(1, per):
            partner(d, v, z).start()

    def got(v, c):
        arrive(v, c)
        for d in range(1, per):
            partner(d, v, c).start()

        @pl.when(v // halves == z)
        def _():
            ship_on(lax.rem(v, halves), c, start)

    def queue_own(n):
        for way in (0, 1):

            @pl.when(n + ahead[way] < units)
            def _():
                own_sends(way, n + ahead[way])

    def gather(n, far):
        @pl.loop(1, cols)
        def _(s):
            lanes = ((0, units - 1 - n, z < mid), (1, n, z >= mid), (0, n, None), (1, units - 1 - n, None))
            for way, v, is_far in lanes:
                if far and is_far is None:
                    continue
                c = z - s if way == 0 else z + s
                there = c >= 0 if way == 0 else c < cols
                if is_far is not None:
                    there = there & (is_far if far else jnp.logical_not(is_far))

                @pl.when(there & awaited(way, v, n))
                def _():
                    got(v, c)

                @pl.when(there & due(way, v, n))
                def _():
                    onward(way, v, c).start()

    def relay_on(h, c, act):
        @pl.when(relays_up)
        def _():
            act(relay(0, h, c), 1)

        @pl.when(relays_down)
        def _():
            act(relay(1, h, c), 0)

    def receive_and_relay(h, c):
        def act(copy, way):
            taken(way, h, c)
            copy.start()

        relay_on(h, c, act)

    def ship_step(h, c):
        v = z * halves + h
        middle = jnp.minimum(v, units - 1 - v)
        below = jnp.where(z >= mid, units - 1 - v, middle)
        above = jnp.where(z < mid, v, middle)
        return jnp.where(c == z, 0, jnp.where(c < z, below, above))

    def relay_due(n):
        def maybe(h, c):
            @pl.when((c >= 0) & (c < cols) & (ship_step(h, c) == n))
            def _():
                receive_and_relay(h, c)

        @pl.loop(0, halves)
        def _(h):
            maybe(h, z)

            @pl.loop(1, cols)
            def _(s):
                maybe(h, z - s)
                maybe(h, z + s)

    def scale(way, source):
        rows_of = wgt.shape[2] // halves
        for h in range(halves):

            @pl.loop(0, cols)
            def _(c):
                wgt[way, c, h * rows_of : (h + 1) * rows_of] = (source(h, c).astype(jnp.float32) * occ_ref[c]).astype(jnp.bfloat16)

    def prepare_away(way):
        present, waited = ((lower, relays_down), (upper, relays_up))[way]

        @pl.when(present)
        def _():
            @pl.when(jnp.logical_not(waited))
            def _():
                @pl.loop(0, halves)
                def _(h):
                    @pl.loop(0, cols)
                    def _(c):
                        taken(way, h, c)

            scale(way, lambda h, c: raw[way, h, c])

    def prepare_home():
        scale(2, lambda h, c: gat[k, z * halves + h, c])

    def answer(t):
        low = t < place
        other = jnp.where(low, t, t + 1)
        slot = jnp.where(low, size + other - place, other - place - size) + W - 1
        near = (slot >= 0) & (slot < 2 * W - 1)
        return low, other, slot, near

    def reply(t, h):
        low, other, slot, near = answer(t)
        there = lax.rem(jnp.where(low, row - per, row + per) + rows, rows)
        go = near & jnp.where(low, row - per >= 0, row + per < rows)
        slot = jnp.clip(slot, 0, 2 * W - 2)
        return go, remote(res.at[t, h], out_ref.at[slot, h], osem.at[t], qsem.at[slot], (there, z))

    def bend(way, t, h):
        there = lax.rem(row + (4 * way - 2) * per + 2 * rows, rows)
        return remote(res.at[t, h], hop.at[t, h], osem.at[t], hsem.at[t, h], (there, z))

    def carry(way, t, h):
        low, other, slot, near = answer(t)
        there = lax.rem(row + (1 - 2 * way) * per + rows, rows)
        slot = jnp.clip(slot, 0, 2 * W - 2)
        go = carries[way] & near & (low if way == 0 else jnp.logical_not(low))
        return go, remote(hop.at[t, h], out_ref.at[slot, h], ssem.at[t], qsem.at[slot], (there, z))

    def bent(m):
        return lax.rem(m, 2) == 0

    def unit(n):
        return jnp.where(z < mid, n, units - 1 - n)

    def product(way, kk, v, target):
        total = jnp.zeros(target.shape, jnp.float32)
        for c in range(cols):
            total = total + lax.dot_general(
                wgt[way, c], gat[kk, v, c], (((1,), (1,)), ((), ())), preferred_element_type=jnp.float32
            )
        target[...] = total.astype(jnp.bfloat16)

    def home(kk, m):
        v = unit(m)
        slot = kk * cols + v // halves - place + W - 1

        @pl.when((slot >= 0) & (slot < 2 * W - 1))
        def _():
            product(2, kk, v, out_ref.at[jnp.clip(slot, 0, 2 * W - 2), lax.rem(v, halves)])

    def home_all(m):
        @pl.loop(0, per)
        def _(kk):
            home(kk, m)

    def away(way, kk, m):
        v = unit(m)
        other = kk * cols + v // halves
        t = jnp.clip(other - way, 0, size - 2)
        go, copy = reply(t, lax.rem(v, halves))

        @pl.when(go & ((other < place) if way == 0 else (other > place)))
        def _():
            product(way, kk, v, res.at[t, lax.rem(v, halves)])
            bends_now = bends[way] & bent(m)

            @pl.when(bends_now)
            def _():
                bend(way, t, lax.rem(v, halves)).start()

            @pl.when(jnp.logical_not(bends_now))
            def _():
                copy.start()

    def carry_due(n):
        def one(m):
            v = unit(m)
            h = lax.rem(v, halves)
            for way in (0, 1):

                @pl.loop(0, per)
                def _(kk):
                    other = kk * cols + v // halves
                    t = jnp.clip(other - way, 0, size - 2)
                    go, copy = carry(way, t, h)

                    @pl.when(go & ((other < place) if way == 0 else (other > place)) & bent(m))
                    def _():
                        remote(hop.at[t, h], hop.at[t, h], xsem.at[0], hsem.at[t, h], (row, z)).wait_recv()
                        copy.start()

        @pl.when(n > bend_step)
        def _():
            @pl.loop(jnp.where(n == bend_step + 1, 0, n - 1), n)
            def _(m):
                one(m)

    def work(n, since, prepare, each):
        if prepare is not None:

            @pl.when(n == since)
            def _():
                prepare()

        @pl.when(n >= since)
        def _():
            @pl.loop(jnp.where(n == since, 0, n), n + 1)
            def _(m):
                each(m)

    gather(0, True)

    @pl.loop(0, units)
    def _(n):
        @pl.when(edge)
        def _():
            carry_due(n)

        queue_own(n)
        gather(n, False)

        @pl.when(n + 1 < units)
        def _():
            gather(n + 1, True)

        @pl.when(jnp.logical_not(edge))
        def _():
            carry_due(n)

        for d in range(per):
            kk = lax.rem(k + d, per)
            if d > 0:
                arrive_whole(kk, unit(n))

            for way in (0, 1):
                ready = functools.partial(prepare_away, way) if d == 0 else None
                work(n, away_step[way], ready, lambda m: away(way, kk, m))

        work(n, own_done, prepare_home, home_all)
        relay_due(n)

    carry_due(units)

    @pl.loop(0, cols)
    def _(c):
        @pl.when((z < cols - 1) & (c <= z))
        def _():
            sent_whole(gat.at[k, :, c], fsem.at[0, c])

        @pl.when((z > 0) & (c >= z))
        def _():
            sent_whole(gat.at[k, :, c], fsem.at[1, c])

    for d in range(1, per):
        sent_whole(gat.at[k], psem.at[d - 1])

    for way, shipped, relayed in ((0, ships_up, relays_up), (1, ships_down, relays_down)):

        @pl.when(shipped)
        def _():
            sent_whole(raw.at[way], xsem.at[way])

        @pl.when(relayed)
        def _():
            sent_whole(raw.at[way], ysem)

    @pl.loop(0, size - 1)
    def _(t):
        low, other, slot, near = answer(t)
        slot = jnp.clip(slot, 0, 2 * W - 2)

        @pl.when(near & jnp.where(low, has_down, has_up))
        def _():
            sent_whole(res.at[t], osem.at[t])

        @pl.when(near & jnp.where(low, carries[0], carries[1]))
        def _():
            sent_whole(hop.at[t, : halves // 2], ssem.at[t])

        @pl.when(near & jnp.where(low, has_up, has_down))
        def _():
            remote(out_ref.at[slot], out_ref.at[slot], xsem.at[0], qsem.at[slot], (row, z)).wait_recv()


def place_blocks(neighbours_ref, counts_ref, block_ref, out_ref, blank, out_sem):
    here = lax.axis_index("row") * lax.axis_size("col") + lax.axis_index("col")
    halves, wide = block_ref.shape[1], block_ref.shape[3]
    blank[...] = jnp.zeros_like(blank)

    def store(j, h):
        at = jnp.clip(neighbours_ref[0, j] - here + (W - 1), 0, 2 * W - 2)
        return pltpu.make_async_copy(block_ref.at[at, h], out_ref.at[j, :, pl.ds(h * wide, wide)], out_sem.at[j])

    slots = out_ref.shape[0]
    for j in range(slots):

        @pl.when(j < counts_ref[0])
        def _():
            for h in range(halves):
                store(j, h).start()

        @pl.when(j >= counts_ref[0])
        def _():
            pltpu.make_async_copy(blank, out_ref.at[j], out_sem.at[j]).start()

    for j in range(slots):
        pltpu.make_async_copy(blank, out_ref.at[j], out_sem.at[j]).wait()


def shards(coeffs, occupations, block_order, neighbours, counts):
    rows, cols = lax.axis_size("row"), lax.axis_size("col")
    states = coeffs.shape[1]
    depth = coeffs.shape[0] // cols
    per = -(-W // cols)
    size = per * cols
    units, half = cols * HALVES, depth // HALVES
    slots_total = 2 * W - 1
    own = coeffs.reshape(cols, depth, states)
    occ = occupations.reshape(cols, 1, states)
    dma = pltpu.SemaphoreType.DMA
    blocks = pl.pallas_call(
        functools.partial(kernel, rows, cols, per),
        out_shape=jax.ShapeDtypeStruct((slots_total, HALVES, depth, half), jnp.bfloat16),
        in_specs=[
            pl.BlockSpec(memory_space=pltpu.HBM),
            pl.BlockSpec(memory_space=pltpu.HBM),
            pl.BlockSpec(memory_space=pltpu.HBM),
        ],
        out_specs=pl.BlockSpec(memory_space=pltpu.VMEM),
        scratch_shapes=[
            pltpu.SMEM(block_order.shape, block_order.dtype),
            pltpu.VMEM(occ.shape, occ.dtype),
            pltpu.VMEM((cols, depth, states), jnp.bfloat16),
            pltpu.VMEM((per, units, cols, half, states), jnp.bfloat16),
            pltpu.VMEM((2, HALVES, cols, half, states), jnp.bfloat16),
            pltpu.VMEM((3, cols, depth, states), jnp.bfloat16),
            pltpu.VMEM((size - 1, HALVES, depth, half), jnp.bfloat16),
            pltpu.VMEM((size - 1, HALVES, depth, half), jnp.bfloat16),
            dma,
            dma,
            dma((units,)),
            dma((2, cols)),
            dma((max(per - 1, 1),)),
            dma((units, cols)),
            dma((per, units)),
            dma((2,)),
            dma,
            dma((2, HALVES, cols)),
            dma((size - 1,)),
            dma((slots_total,)),
            dma((size - 1, HALVES)),
            dma((size - 1,)),
        ],
        compiler_params=pltpu.CompilerParams(
            collective_id=0, has_side_effects=True, vmem_limit_bytes=VMEM_MIB * 1024 * 1024
        ),
        name="density_blocks",
    )(*(pltpu.with_memory_space_constraint(x, pltpu.HBM) for x in (own, block_order, occ)))
    slots = neighbours.shape[1]
    placed = pl.pallas_call(
        place_blocks,
        out_shape=jax.ShapeDtypeStruct((slots, depth, depth), jnp.bfloat16),
        in_specs=[
            pl.BlockSpec(memory_space=pltpu.SMEM),
            pl.BlockSpec(memory_space=pltpu.SMEM),
            pl.BlockSpec(memory_space=pltpu.VMEM),
        ],
        out_specs=pl.BlockSpec(memory_space=pl.ANY),
        scratch_shapes=[
            pltpu.VMEM((depth, depth), jnp.bfloat16),
            dma((slots,)),
        ],
        compiler_params=pltpu.CompilerParams(vmem_limit_bytes=16 * 1024 * 1024),
        name="place_blocks",
    )(neighbours, counts, blocks)
    return placed[None]


def solution(mesh):
    return jax.shard_map(
        shards,
        mesh=mesh,
        in_specs=(P("row", "col"), P(), P(), P(("row", "col"), None), P(("row", "col"))),
        out_specs=P(("row", "col"), None, None, None),
        check_vma=False,
    )
```

```python
import functools

import jax
import jax.numpy as jnp
from jax import lax
from jax.experimental import pallas as pl
from jax.experimental.pallas import tpu as pltpu
from jax.sharding import PartitionSpec as P

W = 8
HALVES = 4
VMEM_MIB = 44
MESH = pl.DeviceIdType.MESH


def kernel(rows, cols, per, own_ref, order_in, occ_in, out_ref, order_ref, occ_ref, stage, gat, raw, wgt, res, hop, order_sem, occ_sem, in_sem, fsem, psem, rsem, gsem, xsem, ysem, usem, osem, qsem, hsem, ssem):
    row, z = lax.axis_index("row"), lax.axis_index("col")
    k = lax.rem(row, per)
    base = row - k
    place = k * cols + z
    size = per * cols
    halves = raw.shape[1]
    units = cols * halves
    mid = cols // 2
    has_up, has_down = row + per < rows, row >= per
    has_up2, has_down2 = row + 2 * per < rows, row >= 2 * per
    odd = lax.rem(row // per, 2) == 1
    ships_up = has_up & jnp.logical_not(odd) & ((place > 0) | has_down)
    ships_down = has_down & jnp.where(odd, (place < size - 1) | has_up, (place < size - 1) & jnp.logical_not(has_up))
    relays_up = has_up2 & (place > 0) & jnp.logical_not(odd)
    relays_down = has_down2 & (place < size - 1) & odd
    lower, upper = has_down & (place > 0), has_up & (place < size - 1)
    own_done = (jnp.minimum(z, cols - 1 - z) + 1) * halves - 1
    edge = (z == 0) | (z == cols - 1)
    direct = (odd, jnp.logical_not(odd) | jnp.logical_not(has_up2))
    bends = (jnp.logical_not(odd) & has_down2, odd & has_up2)
    carries = (jnp.logical_not(odd) & has_up2, odd & has_down2)
    bend_step = jnp.minimum(own_done + 2, units - 1)
    away_step = [jnp.minimum(jnp.where(d, own_done + 1, own_done + 2), units - 1) for d in direct]

    def remote(src, dst, send, recv, device):
        return pltpu.make_async_remote_copy(
            src_ref=src, dst_ref=dst, send_sem=send, recv_sem=recv, device_id=device, device_id_type=MESH
        )

    def onward(way, v, c):
        there = lax.rem(z + 1 - 2 * way + cols, cols)
        return remote(gat.at[k, v, c], gat.at[k, v, c], fsem.at[way, c], rsem.at[v, c], (row, there))

    def partner(d, v, c):
        there = base + lax.rem(k + d, per)
        return remote(gat.at[k, v, c], gat.at[k, v, c], psem.at[d - 1], gsem.at[k, v], (there, z))

    def ship(way, h, c):
        there = lax.rem(row + (1 - 2 * way) * per + rows, rows)
        return remote(gat.at[k, z * halves + h, c], raw.at[way, h, c], xsem.at[way], usem.at[way, h, c], (there, z))

    def relay(way, h, c):
        there = lax.rem(row + (2 - 4 * way) * per + 2 * rows, rows)
        return remote(raw.at[1 - way, h, c], raw.at[way, h, c], ysem, usem.at[way, h, c], (there, z))

    def taken(way, h, c):
        remote(raw.at[way, h, c], raw.at[way, h, c], xsem.at[0], usem.at[way, h, c], (row, z)).wait_recv()

    def arrive(v, c):
        remote(gat.at[k, v, c], gat.at[k, v, c], xsem.at[0], rsem.at[v, c], (row, z)).wait_recv()

    def arrive_whole(kk, v):
        remote(gat.at[kk, v], gat.at[kk, v], xsem.at[0], gsem.at[kk, v], (row, z)).wait_recv()

    def sent_whole(ref, sem):
        remote(ref, ref, sem, xsem.at[0], (row, z)).wait_send()

    def ship_on(h, c, act):
        @pl.when(ships_up)
        def _():
            act(ship(0, h, c))

        @pl.when(ships_down)
        def _():
            act(ship(1, h, c))

    def start(copy):
        copy.start()

    order_copy = pltpu.make_async_copy(order_in, order_ref, order_sem)
    occ_copy = pltpu.make_async_copy(occ_in, occ_ref, occ_sem)
    fills = []
    for i in range(cols):
        for h in range(halves):
            part = pl.ds(h * (stage.shape[1] // halves), stage.shape[1] // halves)
            fills.append(pltpu.make_async_copy(own_ref.at[i, part], stage.at[i, part], in_sem.at[i * halves + h]))
    order_copy.start()
    for fill in fills:
        fill.start()
    occ_copy.start()
    barrier = pltpu.get_barrier_semaphore()
    for d in range(1, per):
        pl.semaphore_signal(barrier, inc=1, device_id=(base + lax.rem(k + d, per), z), device_id_type=MESH)

    greeted = per - 1
    for present, step in ((z < cols - 1, 1), (z > 0, -1)):
        greeted = greeted + present.astype(jnp.int32)

        @pl.when(present)
        def _():
            pl.semaphore_signal(barrier, inc=1, device_id=(row, lax.rem(z + step + cols, cols)), device_id_type=MESH)

    for present, step in ((has_up, per), (has_down, -per), (has_up2, 2 * per), (has_down2, -2 * per)):
        greeted = greeted + present.astype(jnp.int32)

        @pl.when(present)
        def _():
            there = lax.rem(row + step + 2 * rows, rows)
            pl.semaphore_signal(barrier, inc=1, device_id=(there, z), device_id_type=MESH)

    order_copy.wait()
    for fill in fills:
        fill.wait()
    occ_copy.wait()

    first = row * cols

    @pl.loop(0, cols)
    def _(i):
        pick = jnp.clip(order_ref[first + i] - first, 0, cols - 1)

        @pl.loop(0, halves)
        def _(h):
            rows_of = stage.shape[1] // halves
            gat[k, i * halves + h, z] = stage[pick, pl.ds(pl.multiple_of(h * rows_of, rows_of), rows_of)]

    pl.semaphore_wait(barrier, greeted)

    def early(n):
        return 2 * n < units - 1

    def due(way, v, n):
        if way == 0:
            return (z < cols - 1) & jnp.where(z + 1 >= mid, v == units - 1 - n, early(n))
        return (z > 0) & jnp.where(z - 1 < mid, v == n, early(n))

    def awaited(way, v, n):
        if way == 0:
            return jnp.where(z >= mid, v == units - 1 - n, early(n))
        return jnp.where(z < mid, v == n, early(n))

    def own_sends(way, m):
        for v in (units - 1 - m, m) if way == 0 else (m, units - 1 - m):

            @pl.when(due(way, v, m))
            def _():
                onward(way, v, z).start()

    ahead = (jnp.where(z == 0, units, z + 2 * (z >= mid)), jnp.where(z == cols - 1, units, cols - 1 - z + 2 * (z < mid)))
    for way in (0, 1):

        @pl.loop(0, jnp.minimum(ahead[way], units))
        def _(m):
            own_sends(way, m)

    @pl.loop(0, halves)
    def _(h):
        ship_on(h, z, start)

    @pl.loop(0, units)
    def _(v):
        for d in range(1, per):
            partner(d, v, z).start()

    def got(v, c):
        arrive(v, c)
        for d in range(1, per):
            partner(d, v, c).start()

        @pl.when(v // halves == z)
        def _():
            ship_on(lax.rem(v, halves), c, start)

    def queue_own(n):
        for way in (0, 1):

            @pl.when(n + ahead[way] < units)
            def _():
                own_sends(way, n + ahead[way])

    def gather(n, far):
        @pl.loop(1, cols)
        def _(s):
            lanes = ((0, units - 1 - n, z < mid), (1, n, z >= mid), (0, n, None), (1, units - 1 - n, None))
            for way, v, is_far in lanes:
                if far and is_far is None:
                    continue
                c = z - s if way == 0 else z + s
                there = c >= 0 if way == 0 else c < cols
                if is_far is not None:
                    there = there & (is_far if far else jnp.logical_not(is_far))

                @pl.when(there & awaited(way, v, n))
                def _():
                    got(v, c)

                @pl.when(there & due(way, v, n))
                def _():
                    onward(way, v, c).start()

    def relay_on(h, c, act):
        @pl.when(relays_up)
        def _():
            act(relay(0, h, c), 1)

        @pl.when(relays_down)
        def _():
            act(relay(1, h, c), 0)

    def receive_and_relay(h, c):
        def act(copy, way):
            taken(way, h, c)
            copy.start()

        relay_on(h, c, act)

    def ship_step(h, c):
        v = z * halves + h
        middle = jnp.minimum(v, units - 1 - v)
        below = jnp.where(z >= mid, units - 1 - v, middle)
        above = jnp.where(z < mid, v, middle)
        return jnp.where(c == z, 0, jnp.where(c < z, below, above))

    def relay_due(n):
        def maybe(h, c):
            @pl.when((c >= 0) & (c < cols) & (ship_step(h, c) == n))
            def _():
                receive_and_relay(h, c)

        @pl.loop(0, halves)
        def _(h):
            maybe(h, z)

            @pl.loop(1, cols)
            def _(s):
                maybe(h, z - s)
                maybe(h, z + s)

    def scale(way, source):
        rows_of = wgt.shape[2] // halves
        for h in range(halves):

            @pl.loop(0, cols)
            def _(c):
                wgt[way, c, h * rows_of : (h + 1) * rows_of] = (source(h, c).astype(jnp.float32) * occ_ref[c]).astype(jnp.bfloat16)

    def prepare_away(way):
        present, waited = ((lower, relays_down), (upper, relays_up))[way]

        @pl.when(present)
        def _():
            @pl.when(jnp.logical_not(waited))
            def _():
                @pl.loop(0, halves)
                def _(h):
                    @pl.loop(0, cols)
                    def _(c):
                        taken(way, h, c)

            scale(way, lambda h, c: raw[way, h, c])

    def prepare_home():
        scale(2, lambda h, c: gat[k, z * halves + h, c])

    def answer(t):
        low = t < place
        other = jnp.where(low, t, t + 1)
        slot = jnp.where(low, size + other - place, other - place - size) + W - 1
        near = (slot >= 0) & (slot < 2 * W - 1)
        return low, other, slot, near

    def reply(t, h):
        low, other, slot, near = answer(t)
        there = lax.rem(jnp.where(low, row - per, row + per) + rows, rows)
        go = near & jnp.where(low, row - per >= 0, row + per < rows)
        slot = jnp.clip(slot, 0, 2 * W - 2)
        return go, remote(res.at[t, h], out_ref.at[slot, h], osem.at[t], qsem.at[slot], (there, z))

    def bend(way, t, h):
        there = lax.rem(row + (4 * way - 2) * per + 2 * rows, rows)
        return remote(res.at[t, h], hop.at[t, h], osem.at[t], hsem.at[t, h], (there, z))

    def carry(way, t, h):
        low, other, slot, near = answer(t)
        there = lax.rem(row + (1 - 2 * way) * per + rows, rows)
        slot = jnp.clip(slot, 0, 2 * W - 2)
        go = carries[way] & near & (low if way == 0 else jnp.logical_not(low))
        return go, remote(hop.at[t, h], out_ref.at[slot, h], ssem.at[t], qsem.at[slot], (there, z))

    def bent(m):
        return lax.rem(m, 2) == 0

    def unit(n):
        return jnp.where(z < mid, n, units - 1 - n)

    def product(way, kk, v, target):
        total = jnp.zeros(target.shape, jnp.float32)
        for c in range(cols):
            total = total + lax.dot_general(
                wgt[way, c], gat[kk, v, c], (((1,), (1,)), ((), ())), preferred_element_type=jnp.float32
            )
        target[...] = total.astype(jnp.bfloat16)

    def home(kk, m):
        v = unit(m)
        slot = kk * cols + v // halves - place + W - 1

        @pl.when((slot >= 0) & (slot < 2 * W - 1))
        def _():
            product(2, kk, v, out_ref.at[jnp.clip(slot, 0, 2 * W - 2), lax.rem(v, halves)])

    def home_all(m):
        @pl.loop(0, per)
        def _(kk):
            home(kk, m)

    def away(way, kk, m):
        v = unit(m)
        other = kk * cols + v // halves
        t = jnp.clip(other - way, 0, size - 2)
        go, copy = reply(t, lax.rem(v, halves))

        @pl.when(go & ((other < place) if way == 0 else (other > place)))
        def _():
            product(way, kk, v, res.at[t, lax.rem(v, halves)])
            bends_now = bends[way] & bent(m)

            @pl.when(bends_now)
            def _():
                bend(way, t, lax.rem(v, halves)).start()

            @pl.when(jnp.logical_not(bends_now))
            def _():
                copy.start()

    def carry_due(n):
        def one(m):
            v = unit(m)
            h = lax.rem(v, halves)
            for way in (0, 1):

                @pl.loop(0, per)
                def _(kk):
                    other = kk * cols + v // halves
                    t = jnp.clip(other - way, 0, size - 2)
                    go, copy = carry(way, t, h)

                    @pl.when(go & ((other < place) if way == 0 else (other > place)) & bent(m))
                    def _():
                        remote(hop.at[t, h], hop.at[t, h], xsem.at[0], hsem.at[t, h], (row, z)).wait_recv()
                        copy.start()

        @pl.when((carries[0] | carries[1]) & (n > bend_step))
        def _():
            @pl.loop(jnp.where(n == bend_step + 1, 0, n - 1), n)
            def _(m):
                one(m)

    def work(n, since, prepare, each):
        if prepare is not None:

            @pl.when(n == since)
            def _():
                prepare()

        @pl.when(n >= since)
        def _():
            @pl.loop(jnp.where(n == since, 0, n), n + 1)
            def _(m):
                each(m)

    gather(0, True)

    @pl.loop(0, units)
    def _(n):
        @pl.when(edge)
        def _():
            carry_due(n)

        queue_own(n)
        gather(n, False)

        @pl.when(n + 1 < units)
        def _():
            gather(n + 1, True)

        @pl.when(jnp.logical_not(edge))
        def _():
            carry_due(n)

        for d in range(per):
            kk = lax.rem(k + d, per)
            if d > 0:
                arrive_whole(kk, unit(n))

            for way in (0, 1):
                ready = functools.partial(prepare_away, way) if d == 0 else None
                work(n, away_step[way], ready, lambda m: away(way, kk, m))

        work(n, own_done, prepare_home, home_all)
        @pl.when((relays_up | relays_down) & (n <= own_done))
        def _():
            relay_due(n)

    carry_due(units)

    @pl.loop(0, cols)
    def _(c):
        @pl.when((z < cols - 1) & (c <= z))
        def _():
            sent_whole(gat.at[k, :, c], fsem.at[0, c])

        @pl.when((z > 0) & (c >= z))
        def _():
            sent_whole(gat.at[k, :, c], fsem.at[1, c])

    for d in range(1, per):
        sent_whole(gat.at[k], psem.at[d - 1])

    for way, shipped, relayed in ((0, ships_up, relays_up), (1, ships_down, relays_down)):

        @pl.when(shipped)
        def _():
            sent_whole(raw.at[way], xsem.at[way])

        @pl.when(relayed)
        def _():
            sent_whole(raw.at[way], ysem)

    @pl.loop(0, size - 1)
    def _(t):
        low, other, slot, near = answer(t)
        slot = jnp.clip(slot, 0, 2 * W - 2)

        @pl.when(near & jnp.where(low, has_down, has_up))
        def _():
            sent_whole(res.at[t], osem.at[t])

        @pl.when(near & jnp.where(low, carries[0], carries[1]))
        def _():
            sent_whole(hop.at[t, : halves // 2], ssem.at[t])

        @pl.when(near & jnp.where(low, has_up, has_down))
        def _():
            remote(out_ref.at[slot], out_ref.at[slot], xsem.at[0], qsem.at[slot], (row, z)).wait_recv()


def place_blocks(neighbours_ref, counts_ref, block_ref, out_ref, blank, out_sem):
    here = lax.axis_index("row") * lax.axis_size("col") + lax.axis_index("col")
    halves, wide = block_ref.shape[1], block_ref.shape[3]
    blank[...] = jnp.zeros_like(blank)

    def store(j, h):
        at = jnp.clip(neighbours_ref[0, j] - here + (W - 1), 0, 2 * W - 2)
        return pltpu.make_async_copy(block_ref.at[at, h], out_ref.at[j, :, pl.ds(h * wide, wide)], out_sem.at[j])

    slots = out_ref.shape[0]
    for j in range(slots):

        @pl.when(j < counts_ref[0])
        def _():
            for h in range(halves):
                store(j, h).start()

        @pl.when(j >= counts_ref[0])
        def _():
            pltpu.make_async_copy(blank, out_ref.at[j], out_sem.at[j]).start()

    for j in range(slots):
        pltpu.make_async_copy(blank, out_ref.at[j], out_sem.at[j]).wait()


def shards(coeffs, occupations, block_order, neighbours, counts):
    rows, cols = lax.axis_size("row"), lax.axis_size("col")
    states = coeffs.shape[1]
    depth = coeffs.shape[0] // cols
    per = -(-W // cols)
    size = per * cols
    units, half = cols * HALVES, depth // HALVES
    slots_total = 2 * W - 1
    own = coeffs.reshape(cols, depth, states)
    occ = occupations.reshape(cols, 1, states)
    dma = pltpu.SemaphoreType.DMA
    blocks = pl.pallas_call(
        functools.partial(kernel, rows, cols, per),
        out_shape=jax.ShapeDtypeStruct((slots_total, HALVES, depth, half), jnp.bfloat16),
        in_specs=[
            pl.BlockSpec(memory_space=pltpu.HBM),
            pl.BlockSpec(memory_space=pltpu.HBM),
            pl.BlockSpec(memory_space=pltpu.HBM),
        ],
        out_specs=pl.BlockSpec(memory_space=pltpu.VMEM),
        scratch_shapes=[
            pltpu.SMEM(block_order.shape, block_order.dtype),
            pltpu.VMEM(occ.shape, occ.dtype),
            pltpu.VMEM((cols, depth, states), jnp.bfloat16),
            pltpu.VMEM((per, units, cols, half, states), jnp.bfloat16),
            pltpu.VMEM((2, HALVES, cols, half, states), jnp.bfloat16),
            pltpu.VMEM((3, cols, depth, states), jnp.bfloat16),
            pltpu.VMEM((size - 1, HALVES, depth, half), jnp.bfloat16),
            pltpu.VMEM((size - 1, HALVES, depth, half), jnp.bfloat16),
            dma,
            dma,
            dma((units,)),
            dma((2, cols)),
            dma((max(per - 1, 1),)),
            dma((units, cols)),
            dma((per, units)),
            dma((2,)),
            dma,
            dma((2, HALVES, cols)),
            dma((size - 1,)),
            dma((slots_total,)),
            dma((size - 1, HALVES)),
            dma((size - 1,)),
        ],
        compiler_params=pltpu.CompilerParams(
            collective_id=0, has_side_effects=True, vmem_limit_bytes=VMEM_MIB * 1024 * 1024
        ),
        name="density_blocks",
    )(*(pltpu.with_memory_space_constraint(x, pltpu.HBM) for x in (own, block_order, occ)))
    slots = neighbours.shape[1]
    placed = pl.pallas_call(
        place_blocks,
        out_shape=jax.ShapeDtypeStruct((slots, depth, depth), jnp.bfloat16),
        in_specs=[
            pl.BlockSpec(memory_space=pltpu.SMEM),
            pl.BlockSpec(memory_space=pltpu.SMEM),
            pl.BlockSpec(memory_space=pltpu.VMEM),
        ],
        out_specs=pl.BlockSpec(memory_space=pl.ANY),
        scratch_shapes=[
            pltpu.VMEM((depth, depth), jnp.bfloat16),
            dma((slots,)),
        ],
        compiler_params=pltpu.CompilerParams(vmem_limit_bytes=16 * 1024 * 1024),
        name="place_blocks",
    )(neighbours, counts, blocks)
    return placed[None]


def solution(mesh):
    return jax.shard_map(
        shards,
        mesh=mesh,
        in_specs=(P("row", "col"), P(), P(), P(("row", "col"), None), P(("row", "col"))),
        out_specs=P(("row", "col"), None, None, None),
        check_vma=False,
    )
```

```python
import functools

import jax
import jax.numpy as jnp
from jax import lax
from jax.experimental import pallas as pl
from jax.experimental.pallas import tpu as pltpu
from jax.sharding import PartitionSpec as P

W = 8
HALVES = 4
VMEM_MIB = 44
MESH = pl.DeviceIdType.MESH


def kernel(rows, cols, per, own_ref, order_in, occ_in, out_ref, order_ref, occ_ref, stage, gat, raw, wgt, res, hop, order_sem, occ_sem, in_sem, fsem, psem, rsem, gsem, xsem, ysem, usem, osem, qsem, hsem, ssem):
    row, z = lax.axis_index("row"), lax.axis_index("col")
    k = lax.rem(row, per)
    base = row - k
    place = k * cols + z
    size = per * cols
    halves = raw.shape[1]
    units = cols * halves
    mid = cols // 2
    has_up, has_down = row + per < rows, row >= per
    has_up2, has_down2 = row + 2 * per < rows, row >= 2 * per
    odd = lax.rem(row // per, 2) == 1
    ships_up = has_up & jnp.logical_not(odd) & ((place > 0) | has_down)
    ships_down = has_down & jnp.where(odd, (place < size - 1) | has_up, (place < size - 1) & jnp.logical_not(has_up))
    relays_up = has_up2 & (place > 0) & jnp.logical_not(odd)
    relays_down = has_down2 & (place < size - 1) & odd
    lower, upper = has_down & (place > 0), has_up & (place < size - 1)
    own_done = (jnp.minimum(z, cols - 1 - z) + 1) * halves - 1
    edge = (z == 0) | (z == cols - 1)
    direct = (odd, jnp.logical_not(odd) | jnp.logical_not(has_up2))
    bends = (jnp.logical_not(odd) & has_down2, odd & has_up2)
    carries = (jnp.logical_not(odd) & has_up2, odd & has_down2)
    bend_step = jnp.minimum(own_done + 2, units - 1)
    away_step = [jnp.minimum(jnp.where(d, own_done + 1, own_done + 2), units - 1) for d in direct]

    def remote(src, dst, send, recv, device):
        return pltpu.make_async_remote_copy(
            src_ref=src, dst_ref=dst, send_sem=send, recv_sem=recv, device_id=device, device_id_type=MESH
        )

    def onward(way, v, c):
        there = lax.rem(z + 1 - 2 * way + cols, cols)
        return remote(gat.at[k, v, c], gat.at[k, v, c], fsem.at[way, c], rsem.at[v, c], (row, there))

    def partner(d, v, c):
        there = base + lax.rem(k + d, per)
        return remote(gat.at[k, v, c], gat.at[k, v, c], psem.at[d - 1], gsem.at[k, v], (there, z))

    def ship(way, h, c):
        there = lax.rem(row + (1 - 2 * way) * per + rows, rows)
        return remote(gat.at[k, z * halves + h, c], raw.at[way, h, c], xsem.at[way], usem.at[way, h, c], (there, z))

    def relay(way, h, c):
        there = lax.rem(row + (2 - 4 * way) * per + 2 * rows, rows)
        return remote(raw.at[1 - way, h, c], raw.at[way, h, c], ysem, usem.at[way, h, c], (there, z))

    def taken(way, h, c):
        remote(raw.at[way, h, c], raw.at[way, h, c], xsem.at[0], usem.at[way, h, c], (row, z)).wait_recv()

    def arrive(v, c):
        remote(gat.at[k, v, c], gat.at[k, v, c], xsem.at[0], rsem.at[v, c], (row, z)).wait_recv()

    def arrive_whole(kk, v):
        remote(gat.at[kk, v], gat.at[kk, v], xsem.at[0], gsem.at[kk, v], (row, z)).wait_recv()

    def sent_whole(ref, sem):
        remote(ref, ref, sem, xsem.at[0], (row, z)).wait_send()

    def ship_on(h, c, act):
        @pl.when(ships_up)
        def _():
            act(ship(0, h, c))

        @pl.when(ships_down)
        def _():
            act(ship(1, h, c))

    def start(copy):
        copy.start()

    order_copy = pltpu.make_async_copy(order_in, order_ref, order_sem)
    occ_copy = pltpu.make_async_copy(occ_in, occ_ref, occ_sem)
    fills = []
    for i in range(cols):
        for h in range(halves):
            part = pl.ds(h * (stage.shape[1] // halves), stage.shape[1] // halves)
            fills.append(pltpu.make_async_copy(own_ref.at[i, part], stage.at[i, part], in_sem.at[i * halves + h]))
    order_copy.start()
    for fill in fills:
        fill.start()
    occ_copy.start()
    barrier = pltpu.get_barrier_semaphore()
    for d in range(1, per):
        pl.semaphore_signal(barrier, inc=1, device_id=(base + lax.rem(k + d, per), z), device_id_type=MESH)

    greeted = per - 1
    for present, step in ((z < cols - 1, 1), (z > 0, -1)):
        greeted = greeted + present.astype(jnp.int32)

        @pl.when(present)
        def _():
            pl.semaphore_signal(barrier, inc=1, device_id=(row, lax.rem(z + step + cols, cols)), device_id_type=MESH)

    for present, step in ((has_up, per), (has_down, -per), (has_up2, 2 * per), (has_down2, -2 * per)):
        greeted = greeted + present.astype(jnp.int32)

        @pl.when(present)
        def _():
            there = lax.rem(row + step + 2 * rows, rows)
            pl.semaphore_signal(barrier, inc=1, device_id=(there, z), device_id_type=MESH)

    order_copy.wait()
    for fill in fills:
        fill.wait()
    occ_copy.wait()

    first = row * cols

    @pl.loop(0, cols)
    def _(i):
        pick = jnp.clip(order_ref[first + i] - first, 0, cols - 1)

        @pl.loop(0, halves)
        def _(h):
            rows_of = stage.shape[1] // halves
            gat[k, i * halves + h, z] = stage[pick, pl.ds(pl.multiple_of(h * rows_of, rows_of), rows_of)]

    pl.semaphore_wait(barrier, greeted)

    def early(n):
        return 2 * n < units - 1

    def due(way, v, n):
        if way == 0:
            return (z < cols - 1) & jnp.where(z + 1 >= mid, v == units - 1 - n, early(n))
        return (z > 0) & jnp.where(z - 1 < mid, v == n, early(n))

    def awaited(way, v, n):
        if way == 0:
            return jnp.where(z >= mid, v == units - 1 - n, early(n))
        return jnp.where(z < mid, v == n, early(n))

    def own_sends(way, m):
        for v in (units - 1 - m, m) if way == 0 else (m, units - 1 - m):

            @pl.when(due(way, v, m))
            def _():
                onward(way, v, z).start()

    ahead = (jnp.where(z == 0, units, z + 2 * (z >= mid)), jnp.where(z == cols - 1, units, cols - 1 - z + 2 * (z < mid)))
    for way in (0, 1):

        @pl.loop(0, jnp.minimum(ahead[way], units))
        def _(m):
            own_sends(way, m)

    @pl.loop(0, halves)
    def _(h):
        ship_on(h, z, start)

    @pl.loop(0, units)
    def _(v):
        for d in range(1, per):
            partner(d, v, z).start()

    def got(v, c):
        arrive(v, c)
        for d in range(1, per):
            partner(d, v, c).start()

        @pl.when(v // halves == z)
        def _():
            ship_on(lax.rem(v, halves), c, start)

    def queue_own(n):
        for way in (0, 1):

            @pl.when(n + ahead[way] < units)
            def _():
                own_sends(way, n + ahead[way])

    def gather(n, far):
        @pl.loop(1, cols)
        def _(s):
            lanes = ((0, units - 1 - n, z < mid), (1, n, z >= mid), (0, n, None), (1, units - 1 - n, None))
            for way, v, is_far in lanes:
                if far and is_far is None:
                    continue
                c = z - s if way == 0 else z + s
                there = c >= 0 if way == 0 else c < cols
                if is_far is not None:
                    there = there & (is_far if far else jnp.logical_not(is_far))

                @pl.when(there & awaited(way, v, n))
                def _():
                    got(v, c)

                @pl.when(there & due(way, v, n))
                def _():
                    onward(way, v, c).start()

    def relay_on(h, c, act):
        @pl.when(relays_up)
        def _():
            act(relay(0, h, c), 1)

        @pl.when(relays_down)
        def _():
            act(relay(1, h, c), 0)

    def receive_and_relay(h, c):
        def act(copy, way):
            taken(way, h, c)
            copy.start()

        relay_on(h, c, act)

    def ship_step(h, c):
        v = z * halves + h
        middle = jnp.minimum(v, units - 1 - v)
        below = jnp.where(z >= mid, units - 1 - v, middle)
        above = jnp.where(z < mid, v, middle)
        return jnp.where(c == z, 0, jnp.where(c < z, below, above))

    def relay_due(n):
        def maybe(h, c):
            @pl.when((c >= 0) & (c < cols) & (ship_step(h, c) == n))
            def _():
                receive_and_relay(h, c)

        @pl.loop(0, halves)
        def _(h):
            maybe(h, z)

            @pl.loop(1, cols)
            def _(s):
                maybe(h, z - s)
                maybe(h, z + s)

    def scale(way, source):
        rows_of = wgt.shape[2] // halves
        for h in range(halves):

            @pl.loop(0, cols)
            def _(c):
                wgt[way, c, h * rows_of : (h + 1) * rows_of] = (source(h, c).astype(jnp.float32) * occ_ref[c]).astype(jnp.bfloat16)

    def prepare_away(way):
        present, waited = ((lower, relays_down), (upper, relays_up))[way]

        @pl.when(present)
        def _():
            @pl.when(jnp.logical_not(waited))
            def _():
                @pl.loop(0, halves)
                def _(h):
                    @pl.loop(0, cols)
                    def _(c):
                        taken(way, h, c)

            scale(way, lambda h, c: raw[way, h, c])

    def prepare_home():
        scale(2, lambda h, c: gat[k, z * halves + h, c])

    def answer(t):
        low = t < place
        other = jnp.where(low, t, t + 1)
        slot = jnp.where(low, size + other - place, other - place - size) + W - 1
        near = (slot >= 0) & (slot < 2 * W - 1)
        return low, other, slot, near

    def reply(t, h):
        low, other, slot, near = answer(t)
        there = lax.rem(jnp.where(low, row - per, row + per) + rows, rows)
        go = near & jnp.where(low, row - per >= 0, row + per < rows)
        slot = jnp.clip(slot, 0, 2 * W - 2)
        return go, remote(res.at[t, h], out_ref.at[slot, h], osem.at[t], qsem.at[slot], (there, z))

    def bend(way, t, h):
        there = lax.rem(row + (4 * way - 2) * per + 2 * rows, rows)
        return remote(res.at[t, h], hop.at[t, h], osem.at[t], hsem.at[t, h], (there, z))

    def carry(way, t, h):
        low, other, slot, near = answer(t)
        there = lax.rem(row + (1 - 2 * way) * per + rows, rows)
        slot = jnp.clip(slot, 0, 2 * W - 2)
        go = carries[way] & near & (low if way == 0 else jnp.logical_not(low))
        return go, remote(hop.at[t, h], out_ref.at[slot, h], ssem.at[t], qsem.at[slot], (there, z))

    def bent(m):
        return lax.rem(m, 2) == 0

    def unit(n):
        return jnp.where(z < mid, n, units - 1 - n)

    def product(way, kk, v, target):
        total = jnp.zeros(target.shape, jnp.float32)
        for c in range(cols):
            total = total + lax.dot_general(
                wgt[way, c], gat[kk, v, c], (((1,), (1,)), ((), ())), preferred_element_type=jnp.float32
            )
        target[...] = total.astype(jnp.bfloat16)

    def home(kk, m):
        v = unit(m)
        slot = kk * cols + v // halves - place + W - 1

        @pl.when((slot >= 0) & (slot < 2 * W - 1))
        def _():
            product(2, kk, v, out_ref.at[jnp.clip(slot, 0, 2 * W - 2), lax.rem(v, halves)])

    def home_all(m):
        @pl.loop(0, per)
        def _(kk):
            home(kk, m)

    def away(way, kk, m):
        v = unit(m)
        other = kk * cols + v // halves
        t = jnp.clip(other - way, 0, size - 2)
        go, copy = reply(t, lax.rem(v, halves))

        @pl.when(go & jnp.where(way == 0, other < place, other > place))
        def _():
            product(way, kk, v, res.at[t, lax.rem(v, halves)])
            bends_now = jnp.where(way == 0, *bends) & bent(m)

            @pl.when(bends_now)
            def _():
                bend(way, t, lax.rem(v, halves)).start()

            @pl.when(jnp.logical_not(bends_now))
            def _():
                copy.start()

    def carry_due(n):
        def one(m):
            v = unit(m)
            h = lax.rem(v, halves)
            for way in (0, 1):

                @pl.loop(0, per)
                def _(kk):
                    other = kk * cols + v // halves
                    t = jnp.clip(other - way, 0, size - 2)
                    go, copy = carry(way, t, h)

                    @pl.when(go & ((other < place) if way == 0 else (other > place)) & bent(m))
                    def _():
                        remote(hop.at[t, h], hop.at[t, h], xsem.at[0], hsem.at[t, h], (row, z)).wait_recv()
                        copy.start()

        @pl.when((carries[0] | carries[1]) & (n > bend_step))
        def _():
            @pl.loop(jnp.where(n == bend_step + 1, 0, n - 1), n)
            def _(m):
                one(m)

    def work(n, since, prepare, each):
        if prepare is not None:

            @pl.when(n == since)
            def _():
                prepare()

        @pl.when(n >= since)
        def _():
            @pl.loop(jnp.where(n == since, 0, n), n + 1)
            def _(m):
                each(m)

    gather(0, True)

    @pl.loop(0, units)
    def _(n):
        @pl.when(edge)
        def _():
            carry_due(n)

        queue_own(n)
        gather(n, False)

        @pl.when(n + 1 < units)
        def _():
            gather(n + 1, True)

        @pl.when(jnp.logical_not(edge))
        def _():
            carry_due(n)

        for d in range(per):
            kk = lax.rem(k + d, per)
            if d > 0:
                arrive_whole(kk, unit(n))

            if d == 0:
                for way in (0, 1):

                    @pl.when(n == away_step[way])
                    def _():
                        prepare_away(way)

            @pl.loop(0, 2)
            def _(way):
                work(n, jnp.where(way == 0, *away_step), None, lambda m: away(way, kk, m))

        work(n, own_done, prepare_home, home_all)
        @pl.when((relays_up | relays_down) & (n <= own_done))
        def _():
            relay_due(n)

    carry_due(units)

    @pl.loop(0, cols)
    def _(c):
        @pl.when((z < cols - 1) & (c <= z))
        def _():
            sent_whole(gat.at[k, :, c], fsem.at[0, c])

        @pl.when((z > 0) & (c >= z))
        def _():
            sent_whole(gat.at[k, :, c], fsem.at[1, c])

    for d in range(1, per):
        sent_whole(gat.at[k], psem.at[d - 1])

    for way, shipped, relayed in ((0, ships_up, relays_up), (1, ships_down, relays_down)):

        @pl.when(shipped)
        def _():
            sent_whole(raw.at[way], xsem.at[way])

        @pl.when(relayed)
        def _():
            sent_whole(raw.at[way], ysem)

    @pl.loop(0, size - 1)
    def _(t):
        low, other, slot, near = answer(t)
        slot = jnp.clip(slot, 0, 2 * W - 2)

        @pl.when(near & jnp.where(low, has_down, has_up))
        def _():
            sent_whole(res.at[t], osem.at[t])

        @pl.when(near & jnp.where(low, carries[0], carries[1]))
        def _():
            sent_whole(hop.at[t, : halves // 2], ssem.at[t])

        @pl.when(near & jnp.where(low, has_up, has_down))
        def _():
            remote(out_ref.at[slot], out_ref.at[slot], xsem.at[0], qsem.at[slot], (row, z)).wait_recv()


def place_blocks(neighbours_ref, counts_ref, block_ref, out_ref, blank, out_sem):
    here = lax.axis_index("row") * lax.axis_size("col") + lax.axis_index("col")
    halves, wide = block_ref.shape[1], block_ref.shape[3]
    blank[...] = jnp.zeros_like(blank)

    def store(j, h):
        at = jnp.clip(neighbours_ref[0, j] - here + (W - 1), 0, 2 * W - 2)
        return pltpu.make_async_copy(block_ref.at[at, h], out_ref.at[j, :, pl.ds(h * wide, wide)], out_sem.at[j])

    slots = out_ref.shape[0]
    for j in range(slots):

        @pl.when(j < counts_ref[0])
        def _():
            for h in range(halves):
                store(j, h).start()

        @pl.when(j >= counts_ref[0])
        def _():
            pltpu.make_async_copy(blank, out_ref.at[j], out_sem.at[j]).start()

    for j in range(slots):
        pltpu.make_async_copy(blank, out_ref.at[j], out_sem.at[j]).wait()


def shards(coeffs, occupations, block_order, neighbours, counts):
    rows, cols = lax.axis_size("row"), lax.axis_size("col")
    states = coeffs.shape[1]
    depth = coeffs.shape[0] // cols
    per = -(-W // cols)
    size = per * cols
    units, half = cols * HALVES, depth // HALVES
    slots_total = 2 * W - 1
    own = coeffs.reshape(cols, depth, states)
    occ = occupations.reshape(cols, 1, states)
    dma = pltpu.SemaphoreType.DMA
    blocks = pl.pallas_call(
        functools.partial(kernel, rows, cols, per),
        out_shape=jax.ShapeDtypeStruct((slots_total, HALVES, depth, half), jnp.bfloat16),
        in_specs=[
            pl.BlockSpec(memory_space=pltpu.HBM),
            pl.BlockSpec(memory_space=pltpu.HBM),
            pl.BlockSpec(memory_space=pltpu.HBM),
        ],
        out_specs=pl.BlockSpec(memory_space=pltpu.VMEM),
        scratch_shapes=[
            pltpu.SMEM(block_order.shape, block_order.dtype),
            pltpu.VMEM(occ.shape, occ.dtype),
            pltpu.VMEM((cols, depth, states), jnp.bfloat16),
            pltpu.VMEM((per, units, cols, half, states), jnp.bfloat16),
            pltpu.VMEM((2, HALVES, cols, half, states), jnp.bfloat16),
            pltpu.VMEM((3, cols, depth, states), jnp.bfloat16),
            pltpu.VMEM((size - 1, HALVES, depth, half), jnp.bfloat16),
            pltpu.VMEM((size - 1, HALVES, depth, half), jnp.bfloat16),
            dma,
            dma,
            dma((units,)),
            dma((2, cols)),
            dma((max(per - 1, 1),)),
            dma((units, cols)),
            dma((per, units)),
            dma((2,)),
            dma,
            dma((2, HALVES, cols)),
            dma((size - 1,)),
            dma((slots_total,)),
            dma((size - 1, HALVES)),
            dma((size - 1,)),
        ],
        compiler_params=pltpu.CompilerParams(
            collective_id=0, has_side_effects=True, vmem_limit_bytes=VMEM_MIB * 1024 * 1024
        ),
        name="density_blocks",
    )(*(pltpu.with_memory_space_constraint(x, pltpu.HBM) for x in (own, block_order, occ)))
    slots = neighbours.shape[1]
    placed = pl.pallas_call(
        place_blocks,
        out_shape=jax.ShapeDtypeStruct((slots, depth, depth), jnp.bfloat16),
        in_specs=[
            pl.BlockSpec(memory_space=pltpu.SMEM),
            pl.BlockSpec(memory_space=pltpu.SMEM),
            pl.BlockSpec(memory_space=pltpu.VMEM),
        ],
        out_specs=pl.BlockSpec(memory_space=pl.ANY),
        scratch_shapes=[
            pltpu.VMEM((depth, depth), jnp.bfloat16),
            dma((slots,)),
        ],
        compiler_params=pltpu.CompilerParams(vmem_limit_bytes=16 * 1024 * 1024),
        name="place_blocks",
    )(neighbours, counts, blocks)
    return placed[None]


def solution(mesh):
    return jax.shard_map(
        shards,
        mesh=mesh,
        in_specs=(P("row", "col"), P(), P(), P(("row", "col"), None), P(("row", "col"))),
        out_specs=P(("row", "col"), None, None, None),
        check_vma=False,
    )
```

```python
import functools

import jax
import jax.numpy as jnp
from jax import lax
from jax.experimental import pallas as pl
from jax.experimental.pallas import tpu as pltpu
from jax.sharding import PartitionSpec as P

W = 8
HALVES = 4
VMEM_MIB = 44
MESH = pl.DeviceIdType.MESH


def kernel(rows, cols, per, own_ref, order_in, occ_in, out_ref, order_ref, occ_ref, stage, gat, raw, wgt, res, hop, order_sem, occ_sem, in_sem, fsem, psem, rsem, gsem, xsem, ysem, usem, osem, qsem, hsem, ssem):
    row, z = lax.axis_index("row"), lax.axis_index("col")
    k = lax.rem(row, per)
    base = row - k
    place = k * cols + z
    size = per * cols
    halves = raw.shape[1]
    units = cols * halves
    mid = cols // 2
    has_up, has_down = row + per < rows, row >= per
    has_up2, has_down2 = row + 2 * per < rows, row >= 2 * per
    odd = lax.rem(row // per, 2) == 1
    ships_up = has_up & jnp.logical_not(odd) & ((place > 0) | has_down)
    ships_down = has_down & jnp.where(odd, (place < size - 1) | has_up, (place < size - 1) & jnp.logical_not(has_up))
    relays_up = has_up2 & (place > 0) & jnp.logical_not(odd)
    relays_down = has_down2 & (place < size - 1) & odd
    lower, upper = has_down & (place > 0), has_up & (place < size - 1)
    own_done = (jnp.minimum(z, cols - 1 - z) + 1) * halves - 1
    edge = (z == 0) | (z == cols - 1)
    direct = (odd, jnp.logical_not(odd) | jnp.logical_not(has_up2))
    bends = (jnp.logical_not(odd) & has_down2, odd & has_up2)
    carries = (jnp.logical_not(odd) & has_up2, odd & has_down2)
    bend_step = jnp.minimum(own_done + 2, units - 1)
    away_step = [jnp.minimum(jnp.where(d, own_done + 1, own_done + 2), units - 1) for d in direct]

    def remote(src, dst, send, recv, device):
        return pltpu.make_async_remote_copy(
            src_ref=src, dst_ref=dst, send_sem=send, recv_sem=recv, device_id=device, device_id_type=MESH
        )

    def onward(way, v, c):
        there = lax.rem(z + 1 - 2 * way + cols, cols)
        return remote(gat.at[k, v, c], gat.at[k, v, c], fsem.at[way, c], rsem.at[v, c], (row, there))

    def partner(d, v, c):
        there = base + lax.rem(k + d, per)
        return remote(gat.at[k, v, c], gat.at[k, v, c], psem.at[d - 1], gsem.at[k, v], (there, z))

    def ship(way, h, c):
        there = lax.rem(row + (1 - 2 * way) * per + rows, rows)
        return remote(gat.at[k, z * halves + h, c], raw.at[way, h, c], xsem.at[way], usem.at[way, h, c], (there, z))

    def relay(way, h, c):
        there = lax.rem(row + (2 - 4 * way) * per + 2 * rows, rows)
        return remote(raw.at[1 - way, h, c], raw.at[way, h, c], ysem, usem.at[way, h, c], (there, z))

    def taken(way, h, c):
        remote(raw.at[way, h, c], raw.at[way, h, c], xsem.at[0], usem.at[way, h, c], (row, z)).wait_recv()

    def arrive(v, c):
        remote(gat.at[k, v, c], gat.at[k, v, c], xsem.at[0], rsem.at[v, c], (row, z)).wait_recv()

    def arrive_whole(kk, v):
        remote(gat.at[kk, v], gat.at[kk, v], xsem.at[0], gsem.at[kk, v], (row, z)).wait_recv()

    def sent_whole(ref, sem):
        remote(ref, ref, sem, xsem.at[0], (row, z)).wait_send()

    def ship_on(h, c, act):
        @pl.when(ships_up)
        def _():
            act(ship(0, h, c))

        @pl.when(ships_down)
        def _():
            act(ship(1, h, c))

    def start(copy):
        copy.start()

    barrier = pltpu.get_barrier_semaphore()
    for d in range(1, per):
        pl.semaphore_signal(barrier, inc=1, device_id=(base + lax.rem(k + d, per), z), device_id_type=MESH)

    greeted = per - 1
    for present, step in ((z < cols - 1, 1), (z > 0, -1)):
        greeted = greeted + present.astype(jnp.int32)

        @pl.when(present)
        def _():
            pl.semaphore_signal(barrier, inc=1, device_id=(row, lax.rem(z + step + cols, cols)), device_id_type=MESH)

    for present, step in ((has_up, per), (has_down, -per), (has_up2, 2 * per), (has_down2, -2 * per)):
        greeted = greeted + present.astype(jnp.int32)

        @pl.when(present)
        def _():
            there = lax.rem(row + step + 2 * rows, rows)
            pl.semaphore_signal(barrier, inc=1, device_id=(there, z), device_id_type=MESH)

    order_copy = pltpu.make_async_copy(order_in, order_ref, order_sem)
    occ_copy = pltpu.make_async_copy(occ_in, occ_ref, occ_sem)
    fills = []
    for i in range(cols):
        for h in range(halves):
            part = pl.ds(h * (stage.shape[1] // halves), stage.shape[1] // halves)
            fills.append(pltpu.make_async_copy(own_ref.at[i, part], stage.at[i, part], in_sem.at[i * halves + h]))
    order_copy.start()
    for fill in fills:
        fill.start()
    occ_copy.start()

    order_copy.wait()
    for fill in fills:
        fill.wait()
    occ_copy.wait()

    first = row * cols

    @pl.loop(0, cols)
    def _(i):
        pick = jnp.clip(order_ref[first + i] - first, 0, cols - 1)

        @pl.loop(0, halves)
        def _(h):
            rows_of = stage.shape[1] // halves
            gat[k, i * halves + h, z] = stage[pick, pl.ds(pl.multiple_of(h * rows_of, rows_of), rows_of)]

    pl.semaphore_wait(barrier, greeted)

    def early(n):
        return 2 * n < units - 1

    def due(way, v, n):
        if way == 0:
            return (z < cols - 1) & jnp.where(z + 1 >= mid, v == units - 1 - n, early(n))
        return (z > 0) & jnp.where(z - 1 < mid, v == n, early(n))

    def awaited(way, v, n):
        if way == 0:
            return jnp.where(z >= mid, v == units - 1 - n, early(n))
        return jnp.where(z < mid, v == n, early(n))

    def own_sends(way, m):
        for v in (units - 1 - m, m) if way == 0 else (m, units - 1 - m):

            @pl.when(due(way, v, m))
            def _():
                onward(way, v, z).start()

    ahead = (jnp.where(z == 0, units, z + 2 * (z >= mid)), jnp.where(z == cols - 1, units, cols - 1 - z + 2 * (z < mid)))
    for way in (0, 1):

        @pl.loop(0, jnp.minimum(ahead[way], units))
        def _(m):
            own_sends(way, m)

    @pl.loop(0, halves)
    def _(h):
        ship_on(h, z, start)

    @pl.loop(0, units)
    def _(v):
        for d in range(1, per):
            partner(d, v, z).start()

    def got(v, c):
        arrive(v, c)
        for d in range(1, per):
            partner(d, v, c).start()

        @pl.when(v // halves == z)
        def _():
            ship_on(lax.rem(v, halves), c, start)

    def queue_own(n):
        for way in (0, 1):

            @pl.when(n + ahead[way] < units)
            def _():
                own_sends(way, n + ahead[way])

    def gather(n, far):
        @pl.loop(1, cols)
        def _(s):
            lanes = ((0, units - 1 - n, z < mid), (1, n, z >= mid), (0, n, None), (1, units - 1 - n, None))
            for way, v, is_far in lanes:
                if far and is_far is None:
                    continue
                c = z - s if way == 0 else z + s
                there = c >= 0 if way == 0 else c < cols
                if is_far is not None:
                    there = there & (is_far if far else jnp.logical_not(is_far))

                @pl.when(there & awaited(way, v, n))
                def _():
                    got(v, c)

                @pl.when(there & due(way, v, n))
                def _():
                    onward(way, v, c).start()

    def relay_on(h, c, act):
        @pl.when(relays_up)
        def _():
            act(relay(0, h, c), 1)

        @pl.when(relays_down)
        def _():
            act(relay(1, h, c), 0)

    def receive_and_relay(h, c):
        def act(copy, way):
            taken(way, h, c)
            copy.start()

        relay_on(h, c, act)

    def ship_step(h, c):
        v = z * halves + h
        middle = jnp.minimum(v, units - 1 - v)
        below = jnp.where(z >= mid, units - 1 - v, middle)
        above = jnp.where(z < mid, v, middle)
        return jnp.where(c == z, 0, jnp.where(c < z, below, above))

    def relay_due(n):
        def maybe(h, c):
            @pl.when((c >= 0) & (c < cols) & (ship_step(h, c) == n))
            def _():
                receive_and_relay(h, c)

        @pl.loop(0, halves)
        def _(h):
            maybe(h, z)

            @pl.loop(1, cols)
            def _(s):
                maybe(h, z - s)
                maybe(h, z + s)

    def scale(way, source):
        rows_of = wgt.shape[2] // halves
        for h in range(halves):

            @pl.loop(0, cols)
            def _(c):
                wgt[way, c, h * rows_of : (h + 1) * rows_of] = (source(h, c).astype(jnp.float32) * occ_ref[c]).astype(jnp.bfloat16)

    def prepare_away(way):
        present, waited = ((lower, relays_down), (upper, relays_up))[way]

        @pl.when(present)
        def _():
            @pl.when(jnp.logical_not(waited))
            def _():
                @pl.loop(0, halves)
                def _(h):
                    @pl.loop(0, cols)
                    def _(c):
                        taken(way, h, c)

            scale(way, lambda h, c: raw[way, h, c])

    def prepare_home():
        scale(2, lambda h, c: gat[k, z * halves + h, c])

    def answer(t):
        low = t < place
        other = jnp.where(low, t, t + 1)
        slot = jnp.where(low, size + other - place, other - place - size) + W - 1
        near = (slot >= 0) & (slot < 2 * W - 1)
        return low, other, slot, near

    def reply(t, h):
        low, other, slot, near = answer(t)
        there = lax.rem(jnp.where(low, row - per, row + per) + rows, rows)
        go = near & jnp.where(low, row - per >= 0, row + per < rows)
        slot = jnp.clip(slot, 0, 2 * W - 2)
        return go, remote(res.at[t, h], out_ref.at[slot, h], osem.at[t], qsem.at[slot], (there, z))

    def bend(way, t, h):
        there = lax.rem(row + (4 * way - 2) * per + 2 * rows, rows)
        return remote(res.at[t, h], hop.at[t, h], osem.at[t], hsem.at[t, h], (there, z))

    def carry(way, t, h):
        low, other, slot, near = answer(t)
        there = lax.rem(row + (1 - 2 * way) * per + rows, rows)
        slot = jnp.clip(slot, 0, 2 * W - 2)
        go = carries[way] & near & (low if way == 0 else jnp.logical_not(low))
        return go, remote(hop.at[t, h], out_ref.at[slot, h], ssem.at[t], qsem.at[slot], (there, z))

    def bent(m):
        return lax.rem(m, 2) == 0

    def unit(n):
        return jnp.where(z < mid, n, units - 1 - n)

    def product(way, kk, v, target):
        total = jnp.zeros(target.shape, jnp.float32)
        for c in range(cols):
            total = total + lax.dot_general(
                wgt[way, c], gat[kk, v, c], (((1,), (1,)), ((), ())), preferred_element_type=jnp.float32
            )
        target[...] = total.astype(jnp.bfloat16)

    def home(kk, m):
        v = unit(m)
        slot = kk * cols + v // halves - place + W - 1

        @pl.when((slot >= 0) & (slot < 2 * W - 1))
        def _():
            product(2, kk, v, out_ref.at[jnp.clip(slot, 0, 2 * W - 2), lax.rem(v, halves)])

    def home_all(m):
        @pl.loop(0, per)
        def _(kk):
            home(kk, m)

    def away(way, kk, m):
        v = unit(m)
        other = kk * cols + v // halves
        t = jnp.clip(other - way, 0, size - 2)
        go, copy = reply(t, lax.rem(v, halves))

        @pl.when(go & ((other < place) if way == 0 else (other > place)))
        def _():
            product(way, kk, v, res.at[t, lax.rem(v, halves)])
            bends_now = bends[way] & bent(m)

            @pl.when(bends_now)
            def _():
                bend(way, t, lax.rem(v, halves)).start()

            @pl.when(jnp.logical_not(bends_now))
            def _():
                copy.start()

    def carry_due(n):
        def one(m):
            v = unit(m)
            h = lax.rem(v, halves)
            for way in (0, 1):

                @pl.loop(0, per)
                def _(kk):
                    other = kk * cols + v // halves
                    t = jnp.clip(other - way, 0, size - 2)
                    go, copy = carry(way, t, h)

                    @pl.when(go & ((other < place) if way == 0 else (other > place)) & bent(m))
                    def _():
                        remote(hop.at[t, h], hop.at[t, h], xsem.at[0], hsem.at[t, h], (row, z)).wait_recv()
                        copy.start()

        @pl.when((carries[0] | carries[1]) & (n > bend_step))
        def _():
            @pl.loop(jnp.where(n == bend_step + 1, 0, n - 1), n)
            def _(m):
                one(m)

    def work(n, since, prepare, each):
        if prepare is not None:

            @pl.when(n == since)
            def _():
                prepare()

        @pl.when(n >= since)
        def _():
            @pl.loop(jnp.where(n == since, 0, n), n + 1)
            def _(m):
                each(m)

    gather(0, True)

    @pl.loop(0, units)
    def _(n):
        @pl.when(edge)
        def _():
            carry_due(n)

        queue_own(n)
        gather(n, False)

        @pl.when(n + 1 < units)
        def _():
            gather(n + 1, True)

        @pl.when(jnp.logical_not(edge))
        def _():
            carry_due(n)

        for d in range(per):
            kk = lax.rem(k + d, per)
            if d > 0:
                arrive_whole(kk, unit(n))

            for way in (0, 1):
                ready = functools.partial(prepare_away, way) if d == 0 else None
                work(n, away_step[way], ready, lambda m: away(way, kk, m))

        work(n, own_done, prepare_home, home_all)
        @pl.when((relays_up | relays_down) & (n <= own_done))
        def _():
            relay_due(n)

    carry_due(units)

    @pl.loop(0, cols)
    def _(c):
        @pl.when((z < cols - 1) & (c <= z))
        def _():
            sent_whole(gat.at[k, :, c], fsem.at[0, c])

        @pl.when((z > 0) & (c >= z))
        def _():
            sent_whole(gat.at[k, :, c], fsem.at[1, c])

    for d in range(1, per):
        sent_whole(gat.at[k], psem.at[d - 1])

    for way, shipped, relayed in ((0, ships_up, relays_up), (1, ships_down, relays_down)):

        @pl.when(shipped)
        def _():
            sent_whole(raw.at[way], xsem.at[way])

        @pl.when(relayed)
        def _():
            sent_whole(raw.at[way], ysem)

    @pl.loop(0, size - 1)
    def _(t):
        low, other, slot, near = answer(t)
        slot = jnp.clip(slot, 0, 2 * W - 2)

        @pl.when(near & jnp.where(low, has_down, has_up))
        def _():
            sent_whole(res.at[t], osem.at[t])

        @pl.when(near & jnp.where(low, carries[0], carries[1]))
        def _():
            sent_whole(hop.at[t, : halves // 2], ssem.at[t])

        @pl.when(near & jnp.where(low, has_up, has_down))
        def _():
            remote(out_ref.at[slot], out_ref.at[slot], xsem.at[0], qsem.at[slot], (row, z)).wait_recv()


def place_blocks(neighbours_ref, counts_ref, block_ref, out_ref, blank, out_sem):
    here = lax.axis_index("row") * lax.axis_size("col") + lax.axis_index("col")
    halves, wide = block_ref.shape[1], block_ref.shape[3]
    blank[...] = jnp.zeros_like(blank)

    def store(j, h):
        at = jnp.clip(neighbours_ref[0, j] - here + (W - 1), 0, 2 * W - 2)
        return pltpu.make_async_copy(block_ref.at[at, h], out_ref.at[j, :, pl.ds(h * wide, wide)], out_sem.at[j])

    slots = out_ref.shape[0]
    for j in range(slots):

        @pl.when(j < counts_ref[0])
        def _():
            for h in range(halves):
                store(j, h).start()

        @pl.when(j >= counts_ref[0])
        def _():
            pltpu.make_async_copy(blank, out_ref.at[j], out_sem.at[j]).start()

    for j in range(slots):
        pltpu.make_async_copy(blank, out_ref.at[j], out_sem.at[j]).wait()


def shards(coeffs, occupations, block_order, neighbours, counts):
    rows, cols = lax.axis_size("row"), lax.axis_size("col")
    states = coeffs.shape[1]
    depth = coeffs.shape[0] // cols
    per = -(-W // cols)
    size = per * cols
    units, half = cols * HALVES, depth // HALVES
    slots_total = 2 * W - 1
    own = coeffs.reshape(cols, depth, states)
    occ = occupations.reshape(cols, 1, states)
    dma = pltpu.SemaphoreType.DMA
    blocks = pl.pallas_call(
        functools.partial(kernel, rows, cols, per),
        out_shape=jax.ShapeDtypeStruct((slots_total, HALVES, depth, half), jnp.bfloat16),
        in_specs=[
            pl.BlockSpec(memory_space=pltpu.HBM),
            pl.BlockSpec(memory_space=pltpu.HBM),
            pl.BlockSpec(memory_space=pltpu.HBM),
        ],
        out_specs=pl.BlockSpec(memory_space=pltpu.VMEM),
        scratch_shapes=[
            pltpu.SMEM(block_order.shape, block_order.dtype),
            pltpu.VMEM(occ.shape, occ.dtype),
            pltpu.VMEM((cols, depth, states), jnp.bfloat16),
            pltpu.VMEM((per, units, cols, half, states), jnp.bfloat16),
            pltpu.VMEM((2, HALVES, cols, half, states), jnp.bfloat16),
            pltpu.VMEM((3, cols, depth, states), jnp.bfloat16),
            pltpu.VMEM((size - 1, HALVES, depth, half), jnp.bfloat16),
            pltpu.VMEM((size - 1, HALVES, depth, half), jnp.bfloat16),
            dma,
            dma,
            dma((units,)),
            dma((2, cols)),
            dma((max(per - 1, 1),)),
            dma((units, cols)),
            dma((per, units)),
            dma((2,)),
            dma,
            dma((2, HALVES, cols)),
            dma((size - 1,)),
            dma((slots_total,)),
            dma((size - 1, HALVES)),
            dma((size - 1,)),
        ],
        compiler_params=pltpu.CompilerParams(
            collective_id=0, has_side_effects=True, vmem_limit_bytes=VMEM_MIB * 1024 * 1024
        ),
        name="density_blocks",
    )(*(pltpu.with_memory_space_constraint(x, pltpu.HBM) for x in (own, block_order, occ)))
    slots = neighbours.shape[1]
    placed = pl.pallas_call(
        place_blocks,
        out_shape=jax.ShapeDtypeStruct((slots, depth, depth), jnp.bfloat16),
        in_specs=[
            pl.BlockSpec(memory_space=pltpu.SMEM),
            pl.BlockSpec(memory_space=pltpu.SMEM),
            pl.BlockSpec(memory_space=pltpu.VMEM),
        ],
        out_specs=pl.BlockSpec(memory_space=pl.ANY),
        scratch_shapes=[
            pltpu.VMEM((depth, depth), jnp.bfloat16),
            dma((slots,)),
        ],
        compiler_params=pltpu.CompilerParams(vmem_limit_bytes=16 * 1024 * 1024),
        name="place_blocks",
    )(neighbours, counts, blocks)
    return placed[None]


def solution(mesh):
    return jax.shard_map(
        shards,
        mesh=mesh,
        in_specs=(P("row", "col"), P(), P(), P(("row", "col"), None), P(("row", "col"))),
        out_specs=P(("row", "col"), None, None, None),
        check_vma=False,
    )
```
